256 devices in a mesh: dp: 128 (over x_lo, z, y, core), space: 2 (over x_hi).
Axes of the slice: x: 4 (x_hi: 2, x_lo: 2; x = x_hi * 2 + x_lo), y: 4, z: 8, core: 2. Of those that a mesh axis runs over, the one named last changes fastest.
Arguments:
- feature_map: bfloat16 [128, 24, 84, 256], P('dp', 'space'), may hold values from -6 to 6
- proposals: int32 [128, 128, 4], P('dp'), may hold values from 0 to 84, as said below
- hidden_weight: bfloat16 [12544, 512], P(None, 'space'), may hold values from -0.0546875 to 0.0546875
- output_weight: bfloat16 [512, 512], P('space'), may hold values from -0.25 to 0.25
- upstream: bfloat16 [128, 128, 512], P('dp'), may hold values from -6 to 6
Outputs:
- hidden_weight_grad: float32 [12544, 512], P('dp', 'space')
- output_weight_grad: float32 [512, 512], P('space')
- feature_grad: float32 [128, 24, 84, 256], P('dp', 'space')
The draws below stay inside these ranges and needn't reach their ends.
Inputs may be any that keep to these rules, and one draw needn't show every extreme that they name: `proposals`: each row holds top, left, bottom, right with top < bottom <= 24 and left < right <= 84.
All inputs are finite; a program needn't handle non-finite values.
Results may differ from the reference program's by a relative error of at most 0.012.
Values may be sent and summed in bfloat16 or wider, within the bound.
A program may use at most 128 MiB of HBM per device.

```python
import jax
import jax.numpy as jnp
from jax import lax

C = 256
POOL = 7
HID = 512
COLS = 84
HALF_ROWS = 12
ROIS = 128
CIN = 12544
IMAGES = 128


def draw_proposals(key, part):
    keys = jax.random.split(jax.random.fold_in(key, 11), 4)
    height_cells = 2 * HALF_ROWS
    top_edge = jax.random.randint(keys[0], (IMAGES, ROIS), 0, height_cells)
    tallness = jax.random.randint(keys[1], (IMAGES, ROIS), 1, height_cells + 1)
    left_edge = jax.random.randint(keys[2], (IMAGES, ROIS), 0, COLS)
    wideness = jax.random.randint(keys[3], (IMAGES, ROIS), 1, COLS + 1)
    bottom_edge = jnp.minimum(top_edge + tallness, height_cells)
    right_edge = jnp.minimum(left_edge + wideness, COLS)
    return jnp.stack([top_edge, left_edge, bottom_edge, right_edge], axis=-1).astype(jnp.int32)


def block_scale(stream_key, dims, pieces, low, largest):
    level, own = 1.0, jax.random.fold_in(stream_key, 6)
    for axis_at, shards_of in pieces:
        draws = jnp.exp(jax.random.uniform(jax.random.fold_in(own, axis_at), (shards_of,), jnp.float32, low / len(pieces), largest / len(pieces)))
        level = level * jnp.repeat(draws, dims[axis_at] // shards_of).reshape([-1 if axis == axis_at else 1 for axis in range(len(dims))])
    return level


def normal_values(rng, extent, scale, bound, cuts=(), dtype=jnp.bfloat16):
    factor_of = block_scale(rng, extent, cuts, -0.22, 0.18) if cuts else 1.0
    values = jax.random.normal(rng, extent, jnp.float32) * scale * factor_of
    return jnp.minimum(jnp.maximum(values, -bound), bound).astype(dtype)


def setup_inputs(seed: int = 0) -> dict:
    streams_of = jax.random.split(jax.random.key(seed), 6)
    return {
        "feature_map": normal_values(streams_of[0], (IMAGES, 2 * HALF_ROWS, COLS, C), 1.0, 6.0, ((0, 128), (1, 2))),
        "proposals": draw_proposals(jax.random.fold_in(streams_of[5], 71), 0),
        "hidden_weight": normal_values(streams_of[2], (CIN, HID), CIN ** -0.5, 0.0546875, ((1, 2),)),
        "output_weight": normal_values(streams_of[3], (HID, HID), HID ** -0.5, 0.25, ((0, 2),)),
        "upstream": normal_values(streams_of[4], (IMAGES, ROIS, HID), 1.0, 6.0, ((0, 128),)),
    }


def axis_weights(low_edge, high_edge, grid_points):
    edge_start = low_edge.astype(jnp.float32)
    bin_size = (high_edge - low_edge).astype(jnp.float32) / POOL
    bin_index = jnp.arange(POOL).astype(jnp.float32)
    offsets = jnp.array([0.25, 0.75], jnp.float32)
    sample_points = edge_start[:, None, None] + (bin_index[None, :, None] + offsets[None, None, :]) * bin_size[:, None, None] - 0.5
    weights = jnp.maximum(0.0, 1.0 - jnp.abs(sample_points[..., None] - grid_points[None, None, None, :]))
    return lax.optimization_barrier(jnp.mean(weights, axis=2))

def activate(values):
    return jax.nn.gelu(values, approximate=True)

def gelu_grad(values, incoming):
    return jax.vjp(activate, values)[1](incoming)[0]

def crop_rows(own_map, row_weight, col_weight):
    height_cells, width_cells, channels = own_map.shape
    proposal_count = row_weight.shape[0]
    flattened = jnp.transpose(own_map, (1, 0, 2)).reshape(width_cells, height_cells * channels)
    across = jnp.dot(col_weight.reshape(proposal_count * POOL, width_cells), flattened, preferred_element_type=jnp.float32)
    across = across.reshape(proposal_count, POOL, height_cells, channels)
    pooled = jnp.einsum('riy,rjyc->rijc', row_weight.astype(jnp.float32), across, precision=lax.Precision.HIGHEST)
    return pooled.reshape(proposal_count, POOL * POOL * channels)

def crop_back(grad_pooled, row_weight, col_weight, channels):
    proposal_count, _, height_cells = row_weight.shape
    width_cells = col_weight.shape[2]
    grad_block = grad_pooled.astype(jnp.float32).reshape(proposal_count, POOL, POOL, channels)
    spread = jnp.einsum('riy,rijc->rjyc', row_weight.astype(jnp.float32), grad_block, precision=lax.Precision.HIGHEST)
    total = lax.dot_general(col_weight.astype(jnp.float32).reshape(proposal_count * POOL, width_cells), spread.reshape(proposal_count * POOL, height_cells * channels), (((0,), (0,)), ((), ())), precision=lax.Precision.HIGHEST, preferred_element_type=jnp.float32)
    return jnp.transpose(total.reshape(width_cells, height_cells, channels), (1, 0, 2))

def reference(feature_map, proposals, hidden_weight, output_weight, upstream):

    def per_image(running, sample):
        own_map, corners, incoming = sample
        height_cells = own_map.shape[0]
        row_weight = axis_weights(corners[:, 0], corners[:, 2], jnp.arange(height_cells).astype(jnp.float32))
        col_weight = axis_weights(corners[:, 1], corners[:, 3], jnp.arange(COLS).astype(jnp.float32)).astype(jnp.bfloat16)
        pooled = crop_rows(own_map, row_weight, col_weight).astype(jnp.bfloat16)
        pre_hidden = jnp.dot(pooled, hidden_weight, preferred_element_type=jnp.float32)
        hidden = activate(pre_hidden).astype(jnp.bfloat16)
        pre_output = jnp.dot(hidden, output_weight, preferred_element_type=jnp.float32)
        output_delta = gelu_grad(pre_output, incoming.astype(jnp.float32)).astype(jnp.bfloat16)
        step_second = lax.dot_general(hidden, output_delta, (((0,), (0,)), ((), ())), preferred_element_type=jnp.float32)
        hidden_back = lax.dot_general(output_delta, output_weight, (((1,), (1,)), ((), ())), preferred_element_type=jnp.float32)
        hidden_delta = gelu_grad(pre_hidden, hidden_back).astype(jnp.bfloat16)
        step_first = lax.dot_general(pooled, hidden_delta, (((0,), (0,)), ((), ())), preferred_element_type=jnp.float32)
        pooled_grad = lax.dot_general(hidden_delta, hidden_weight, (((1,), (1,)), ((), ())), preferred_element_type=jnp.float32)
        map_grad = crop_back(pooled_grad, row_weight, col_weight, own_map.shape[2])
        return ((running[0] + step_first, running[1] + step_second), map_grad)
    start = (jnp.zeros((CIN, HID), jnp.float32), jnp.zeros((HID, HID), jnp.float32))
    totals, feature_grad = lax.scan(per_image, start, (feature_map, proposals, upstream))
    return (totals[0], totals[1], feature_grad)
```

```python
import jax
import jax.numpy as jnp
from jax import lax
from jax.experimental import pallas as pl
from jax.experimental.pallas import tpu as pltpu
from jax.sharding import PartitionSpec as P

MESH = pl.DeviceIdType.MESH
POOL = 7


def copy_for_each(x, axis):
    size = lax.axis_size(axis)
    return lax.all_to_all(jnp.broadcast_to(x[None], (size, *x.shape)), axis, 0, 0, tiled=True)


def joined_along(blocks, dim):
    blocks = jnp.moveaxis(blocks, 0, dim)
    dims = blocks.shape
    return blocks.reshape(*dims[:dim], dims[dim] * dims[dim + 1], *dims[dim + 2 :])


def collect(x, axis, dim):
    blocks = copy_for_each(x, axis)
    return joined_along(blocks, dim)


def over_copies(x, axis):
    return copy_for_each(x, axis).astype(jnp.float32).sum(axis=0)


def in_blocks(x, dim, size):
    before, after = (x.shape[:dim], x.shape[dim + 1 :])
    return jnp.moveaxis(x.reshape(*before, size, -1, *after), dim, 0)


def summed_on_arrival(x, axis, dim):
    blocks = in_blocks(x, dim, lax.axis_size(axis))
    arrived = lax.all_to_all(blocks, axis, split_axis=0, concat_axis=0, tiled=True)
    return arrived.astype(jnp.float32).sum(axis=0)


def axis_weights(low_edge, high_edge, grid_points):
    edge_start = low_edge.astype(jnp.float32)
    bin_size = (high_edge - low_edge).astype(jnp.float32) / POOL
    bin_index = jnp.arange(POOL).astype(jnp.float32)
    offsets = jnp.array([0.25, 0.75], jnp.float32)
    sample_points = (
        edge_start[:, None, None]
        + (bin_index[None, :, None] + offsets[None, None, :]) * bin_size[:, None, None]
        - 0.5
    )
    weights = jnp.maximum(
        0.0, 1.0 - jnp.abs(sample_points[..., None] - grid_points[None, None, None, :])
    )
    return jnp.mean(weights, axis=2)


def activate(values):
    return jax.nn.gelu(values, approximate=True)


def gelu_grad(values, incoming):
    return jax.vjp(activate, values)[1](incoming)[0]


def block_shape(proposal_count):
    block_size = 32
    return (block_size, proposal_count // block_size)


def crop_rows(own_map, row_weight, col_weight):
    height_cells, width_cells, channels = own_map.shape
    proposal_count = row_weight.shape[0]
    block_size, block_count = block_shape(proposal_count)
    flattened = jnp.transpose(own_map, (1, 0, 2)).reshape(width_cells, height_cells * channels)

    def per_block(blocks):
        row_part, col_part = blocks
        across = jnp.dot(
            col_part.reshape(block_size * POOL, width_cells),
            flattened,
            preferred_element_type=jnp.float32,
        )
        across = across.reshape(block_size, POOL, height_cells, channels)
        return jnp.einsum("riy,rjyc->rijc", row_part, across, precision=lax.Precision.HIGHEST)

    pooled = lax.map(
        per_block,
        (
            row_weight.reshape(block_count, block_size, POOL, height_cells),
            col_weight.reshape(block_count, block_size, POOL, width_cells),
        ),
    )
    return pooled.reshape(proposal_count, POOL * POOL * channels)


def crop_back(grad_pooled, row_weight, col_weight, channels):
    proposal_count, _, height_cells = row_weight.shape
    width_cells = col_weight.shape[2]
    block_size, block_count = block_shape(proposal_count)

    def per_block(running, blocks):
        row_part, col_part, grad_part = blocks
        grad_block = grad_part.reshape(block_size, POOL, POOL, channels)
        spread = jnp.einsum("riy,rijc->rjyc", row_part, grad_block, precision=lax.Precision.HIGHEST)
        added = lax.dot_general(
            col_part.astype(jnp.float32).reshape(block_size * POOL, width_cells),
            spread.reshape(block_size * POOL, height_cells * channels),
            (((0,), (0,)), ((), ())),
            precision=lax.Precision.HIGHEST,
            preferred_element_type=jnp.float32,
        )
        return (running + added, None)

    start = jnp.zeros((width_cells, height_cells * channels), jnp.float32)
    blocks = (
        row_weight.reshape(block_count, block_size, POOL, height_cells),
        col_weight.reshape(block_count, block_size, POOL, width_cells),
        grad_pooled.reshape(block_count, block_size, grad_pooled.shape[1]),
    )
    total, _ = lax.scan(per_block, start, blocks)
    return jnp.transpose(total.reshape(width_cells, height_cells, channels), (1, 0, 2))


def place():
    me = lax.axis_index("dp")
    return me // 64, (me // 8) % 8, (me // 2) % 4, me % 2


def index_of(x, z, y, c):
    return ((x * 8 + z) * 4 + y) * 2 + c


def chains_of(hops):
    return ((0, 1, hops), (1, -1, hops), (0, -1, hops - 1), (1, 1, hops - 1))


def reduce_kernel(
    s_ref, first_ref, second_ref,
    za_s, za_r, yb_s, yb_r, ya_s, ya_r, zb_s, zb_r, x_s, x_r, c_s, c_r, gather,
    acc_a, acc_b, mid_a, mid_b, final,
    za_ss, za_rs, yb_ss, yb_rs, ya_ss, ya_rs, zb_ss, zb_rs, xc_ss, xc_rs, g_ss, g_rs,
):
    x, z, y, c = place()

    def at_z(step):
        return {"dp": index_of(x, (z + step + 8) % 8, y, c)}

    def at_y(step):
        return {"dp": index_of(x, z, (y + step + 4) % 4, c)}

    at_x = {"dp": index_of(1 - x, z, y, c)}
    at_c = {"dp": index_of(x, z, y, 1 - c)}

    barrier = pltpu.get_barrier_semaphore()
    peers = [at_z(k) for k in range(1, 8)] + [at_y(k) for k in range(1, 4)] + [at_x, at_c]
    for peer in peers:
        pl.semaphore_signal(barrier, inc=1, device_id=peer, device_id_type=MESH)
    pl.semaphore_wait(barrier, len(peers))

    copies = []

    def ring(size, pos, to, own, send, recv, ssem, rsem):
        chains = chains_of(size // 2)
        live = {}

        def slot(k, h):
            return sum(ch[2] for ch in chains[:k]) + h

        def go(k, h):
            u, way, hops = chains[k]
            if h > 0:
                live[k, h - 1].wait_recv()
            dest = (pos + way * (hops - h) + size) % size
            value = own(u, dest)
            if h > 0:
                value = value + recv[slot(k, h - 1)].astype(jnp.float32)
            at = slot(k, h)
            send[at] = value.astype(jnp.bfloat16)
            live[k, h] = pltpu.make_async_remote_copy(
                src_ref=send.at[at], dst_ref=recv.at[at], send_sem=ssem.at[at], recv_sem=rsem.at[at],
                device_id=to(way), device_id_type=MESH,
            )
            live[k, h].start()
            copies.append(live[k, h])

        def total(u):
            value = own(u, pos)
            for k, (piece, _, hops) in enumerate(chains):
                if piece == u and hops > 0:
                    live[k, hops - 1].wait_recv()
                    value = value + recv[slot(k, hops - 1)].astype(jnp.float32)
            return value

        return go, total

    za_go, za_total = ring(8, z, at_z, lambda u, d: s_ref[u, d, :, 0:96, :], za_s, za_r, za_ss, za_rs)
    yb_go, yb_total = ring(4, y, at_y, lambda u, d: s_ref[u, :, d, 96:208, :], yb_s, yb_r, yb_ss, yb_rs)
    ya_go, ya_total = ring(4, y, at_y, lambda u, d: acc_a[u, d], ya_s, ya_r, ya_ss, ya_rs)
    zb_go, zb_total = ring(8, z, at_z, lambda u, d: acc_b[u, d], zb_s, zb_r, zb_ss, zb_rs)

    for k in (0, 1):
        za_go(k, 0)
    for k in (0, 1):
        yb_go(k, 0)
    for k in (2, 3):
        za_go(k, 0)
    for k in (2, 3):
        yb_go(k, 0)
    for k in (0, 1, 2, 3):
        za_go(k, 1)
    for k in (0, 1):
        yb_go(k, 1)
    for k in (0, 1, 2, 3):
        za_go(k, 2)
    for k in (0, 1):
        za_go(k, 3)
    for u in (0, 1):
        acc_a[u] = za_total(u)
        ya_go(u, 0)
    for k in (2, 3):
        ya_go(k, 0)
    for u in (0, 1):
        acc_b[u] = yb_total(u)
        zb_go(u, 0)
    for k in (2, 3):
        zb_go(k, 0)
    for k in (0, 1):
        ya_go(k, 1)
    for k in (0, 1, 2, 3):
        zb_go(k, 1)
    for u in (0, 1):
        mid_a[u] = ya_total(u)
    for k in (0, 1, 2, 3):
        zb_go(k, 2)
    for k in (0, 1):
        zb_go(k, 3)
    for u in (0, 1):
        mid_b[u] = zb_total(u)

    def one(src, dst, ssem, rsem, peer):
        copy = pltpu.make_async_remote_copy(
            src_ref=src, dst_ref=dst, send_sem=ssem, recv_sem=rsem, device_id=peer, device_id_type=MESH
        )
        copy.start()
        copies.append(copy)
        return copy

    x_s[0:96] = mid_a[1 - x].astype(jnp.bfloat16)
    x_s[96:208] = mid_b[1 - x].astype(jnp.bfloat16)
    across = one(x_s, x_r, xc_ss.at[0], xc_rs.at[0], at_x)
    across.wait_recv()
    final[0:96] = mid_a[x] + x_r[0:96].astype(jnp.float32)
    final[96:208] = mid_b[x] + x_r[96:208].astype(jnp.float32)

    gather[c, x, z, y] = final[0:8]
    mine = gather.at[c, x, z, y]
    steps = [one(mine, mine, g_ss.at[k], g_rs.at[k], at_z(k)) for k in range(1, 8)]
    low, high = final[8:106], final[106:204]
    c_s[...] = jnp.where(c == 0, high, low)
    swap = one(c_s, c_r, xc_ss.at[1], xc_rs.at[1], at_c)
    swap.wait_recv()
    kept = jnp.where(c == 0, low, high)
    got = c_r[...]
    first_ref[:, 0:128] = jnp.where(c == 0, kept, got)
    first_ref[:, 128:256] = jnp.where(c == 0, got, kept)
    for step in steps:
        step.wait_recv()
    steps = []
    for k in range(1, 4):
        column = gather.at[c, x, :, y]
        steps.append(one(column, column, g_ss.at[7 + k], g_rs.at[7 + k], at_y(k)))
    for step in steps:
        step.wait_recv()
    plane = gather.at[c, x]
    one(plane, plane, g_ss.at[11], g_rs.at[11], at_x).wait_recv()
    half = gather.at[c]
    one(half, half, g_ss.at[12], g_rs.at[12], at_c).wait_recv()
    for k in range(2):
        for u in range(2):
            at = k * 256 + u * 128
            second_ref[:, at:at + 128] = gather[k, u].reshape(256, 128)
    for copy in copies:
        copy.wait_send()


def reduce_all(s):
    bf, f32 = jnp.bfloat16, jnp.float32
    dma = pltpu.SemaphoreType.DMA
    return pl.pallas_call(
        reduce_kernel,
        out_shape=(jax.ShapeDtypeStruct((98, 256), f32), jax.ShapeDtypeStruct((256, 512), f32)),
        in_specs=[pl.BlockSpec(memory_space=pltpu.VMEM)],
        out_specs=[pl.BlockSpec(memory_space=pltpu.VMEM)] * 2,
        scratch_shapes=[
            pltpu.VMEM((14, 4, 96, 128), bf), pltpu.VMEM((14, 4, 96, 128), bf),
            pltpu.VMEM((6, 8, 112, 128), bf), pltpu.VMEM((6, 8, 112, 128), bf),
            pltpu.VMEM((6, 96, 128), bf), pltpu.VMEM((6, 96, 128), bf),
            pltpu.VMEM((14, 112, 128), bf), pltpu.VMEM((14, 112, 128), bf),
            pltpu.VMEM((208, 128), bf), pltpu.VMEM((208, 128), bf),
            pltpu.VMEM((98, 128), f32), pltpu.VMEM((98, 128), f32),
            pltpu.VMEM((2, 2, 8, 4, 8, 128), f32),
            pltpu.VMEM((2, 4, 96, 128), f32), pltpu.VMEM((2, 8, 112, 128), f32),
            pltpu.VMEM((2, 96, 128), f32), pltpu.VMEM((2, 112, 128), f32),
            pltpu.VMEM((208, 128), f32),
            dma((14,)), dma((14,)), dma((6,)), dma((6,)), dma((6,)), dma((6,)), dma((14,)), dma((14,)),
            dma((2,)), dma((2,)), dma((13,)), dma((13,)),
        ],
        compiler_params=pltpu.CompilerParams(collective_id=1, has_side_effects=True, vmem_limit_bytes=60 * 1024 * 1024),
        name="reduce_all",
    )(s)


def on_device(feature_map, proposals, hidden_weight, output_weight, upstream):
    own_map = feature_map[0]
    corners = proposals[0]
    own_height = own_map.shape[0]
    map_width = own_map.shape[1]
    channels = own_map.shape[2]
    col_weight = axis_weights(
        corners[:, 1], corners[:, 3], jnp.arange(map_width, dtype=jnp.int32).astype(jnp.float32)
    ).astype(jnp.bfloat16)
    full_grid = jnp.arange(own_height * lax.axis_size("space"), dtype=jnp.int32).astype(jnp.float32)
    full_weight = axis_weights(corners[:, 0], corners[:, 2], full_grid)
    whole_map = collect(own_map, "space", 0)
    pooled = crop_rows(whole_map, full_weight, col_weight).astype(jnp.bfloat16)
    pre_hidden = jnp.dot(pooled, hidden_weight, preferred_element_type=jnp.float32)
    hidden = activate(pre_hidden).astype(jnp.bfloat16)
    pre_output = over_copies(
        jnp.dot(hidden, output_weight, preferred_element_type=jnp.float32).astype(jnp.bfloat16),
        "space",
    ).astype(jnp.float32)
    output_delta = gelu_grad(pre_output, upstream[0].astype(jnp.float32)).astype(jnp.bfloat16)
    hidden_back = lax.dot_general(
        output_delta, output_weight, (((1,), (1,)), ((), ())), preferred_element_type=jnp.float32
    )
    hidden_delta = gelu_grad(pre_hidden, hidden_back).astype(jnp.bfloat16)
    core = lax.axis_index("dp") % 2

    def half_of(array, which, width):
        return lax.dynamic_slice_in_dim(array, which * width, width, 1)

    def swapped(array):
        return lax.ppermute(array, "dp", [(k, k ^ 1) for k in range(128)])

    def both(left, right, width):
        own = lax.dot_general(
            left, half_of(right, core, width), (((0,), (0,)), ((), ())), preferred_element_type=jnp.float32
        )
        other = lax.dot_general(
            swapped(left), swapped(half_of(right, 1 - core, width)), (((0,), (0,)), ((), ())),
            preferred_element_type=jnp.float32,
        )
        return own + other

    step_first = both(pooled, hidden_delta, 128)
    step_second = both(hidden, output_delta, 256)
    chunks = jnp.concatenate(
        [
            jnp.transpose(step_second.reshape(256, 2, 128), (1, 0, 2)).reshape(64, 8, 128),
            step_first.reshape(64, 196, 128),
            jnp.zeros((64, 4, 128), jnp.float32),
        ],
        axis=1,
    )
    first_total, second_total = reduce_all(chunks.reshape(2, 8, 4, 208, 128))
    partial_grad = lax.dot_general(
        hidden_delta, hidden_weight, (((1,), (1,)), ((), ())), preferred_element_type=jnp.float32
    )
    whole_grad = crop_back(partial_grad, full_weight, col_weight, channels)
    map_grad = summed_on_arrival(whole_grad.astype(jnp.bfloat16), "space", 0)
    return (first_total, second_total, map_grad[None])


def solution(mesh):
    placed = (
        P("dp", "space", None, None),
        P("dp", None, None),
        P(None, "space"),
        P("space", None),
        P("dp", None, None),
    )
    return jax.shard_map(
        on_device,
        mesh=mesh,
        in_specs=placed,
        out_specs=(P("dp", "space"), P("space", None), P("dp", "space", None, None)),
        check_vma=False,
    )
```

```python
import jax
import jax.numpy as jnp
from jax import lax
from jax.experimental import pallas as pl
from jax.experimental.pallas import tpu as pltpu
from jax.sharding import PartitionSpec as P

MESH = pl.DeviceIdType.MESH
POOL = 7
ROIS = 128
CHANNELS = 256
ROWS = 12
COLS = 84
PITCH = 96
HALF = ROWS * PITCH
BINS = POOL * ROIS
WIDE = POOL * CHANNELS
BF = jnp.bfloat16
F32 = jnp.float32
TN = (((0,), (0,)), ((), ()))
NT = (((1,), (1,)), ((), ()))
SCALE = 0.7978845608028654
CUBIC = 0.044715


def gelu_of(v):
    return 0.5 * v * (1.0 + jnp.tanh(SCALE * (v + CUBIC * v * v * v)))


def gelu_slope(v):
    t = jnp.tanh(SCALE * (v + CUBIC * v * v * v))
    return 0.5 * (1.0 + t) + 0.5 * v * (1.0 - t * t) * (SCALE * (1.0 + 3.0 * CUBIC * v * v))


def place():
    me = lax.axis_index("dp")
    return me // 64, (me // 8) % 8, (me // 2) % 4, me % 2


def index_of(x, z, y, c):
    return ((x * 8 + z) * 4 + y) * 2 + c


def chains_of(hops):
    return ((0, 1, hops), (1, -1, hops), (0, -1, hops - 1), (1, 1, hops - 1))


def step_kernel(
    fm_ref, corner_ref, hw_hbm, ow_ref, up_ref, first_ref, second_ref, map_ref,
    hw_ref, feat, far, row_all, col_all, weights, pooled, hid_acc,
    z_s, z_r, hd_own, hd_pair, hd_s, od_pair, od_s, hid_pair, s_flat, chunks, grads, map_acc, map_s, map_r,
    za_s, za_r, yb_s, yb_r, ya_s, ya_r, zb_s, zb_r, x_s, x_r, c_s, c_r, gather,
    acc_a, acc_b, mid_a, mid_b, final,
    hw_sem, f_sem, p_ss, p_rs, m_ss, m_rs,
    za_ss, za_rs, yb_ss, yb_rs, ya_ss, ya_rs, zb_ss, zb_rs, xc_ss, xc_rs, g_ss, g_rs,
):
    x, z, y, c = place()
    s = lax.axis_index("space")

    def at_z(step):
        return {"dp": index_of(x, (z + step + 8) % 8, y, c)}

    def at_y(step):
        return {"dp": index_of(x, z, (y + step + 4) % 4, c)}

    at_x = {"dp": index_of(1 - x, z, y, c)}
    at_c = {"dp": index_of(x, z, y, 1 - c)}
    at_s = {"space": 1 - s}

    load_hw = pltpu.make_async_copy(hw_hbm, hw_ref, hw_sem)
    load_hw.start()
    barrier = pltpu.get_barrier_semaphore()
    peers = [at_s, at_c] + [at_z(k) for k in range(1, 8)] + [at_y(k) for k in range(1, 4)] + [at_x]
    for peer in peers:
        pl.semaphore_signal(barrier, inc=1, device_id=peer, device_id_type=MESH)
    pl.semaphore_wait(barrier, len(peers))

    copies = []

    def one(src, dst, ssem, rsem, peer):
        copy = pltpu.make_async_remote_copy(
            src_ref=src, dst_ref=dst, send_sem=ssem, recv_sem=rsem, device_id=peer, device_id_type=MESH
        )
        copy.start()
        copies.append(copy)
        return copy

    features = one(fm_ref, far, f_sem.at[0], f_sem.at[1], at_s)

    feat[...] = jnp.zeros((2 * HALF, CHANNELS), BF)
    for row in range(ROWS):
        feat[row * PITCH:row * PITCH + COLS] = fm_ref[row]
    lane = lax.broadcasted_iota(jnp.int32, (ROIS, 128), 1).astype(F32)
    base = (ROWS * s).astype(F32)
    row_at = jnp.where(lane < ROWS, lane + base, lane - base)
    spot = lax.broadcasted_iota(jnp.int32, (128, 2 * HALF), 1).astype(F32)
    slot_at = lax.broadcasted_iota(jnp.int32, (128, 2 * HALF), 0).astype(F32)
    row_of = jnp.floor((spot + 0.5) * (1.0 / PITCH))
    row_pick = (row_of == slot_at).astype(F32).astype(BF)
    col_pick = jnp.logical_and(spot - row_of * PITCH == slot_at, slot_at < COLS).astype(F32).astype(BF)

    def bins(low, high, grid, k):
        start = corner_ref[:, low:low + 1].astype(F32)
        size = (corner_ref[:, high:high + 1] - corner_ref[:, low:low + 1]).astype(F32) / POOL
        total = jnp.zeros((ROIS, 128), F32)
        for offset in (0.25, 0.75):
            point = start + (k + offset) * size - 0.5
            total = total + jnp.maximum(0.0, 1.0 - jnp.abs(point - grid))
        return (0.5 * total).astype(BF)

    for k in range(POOL):
        row_all[k] = jnp.dot(bins(0, 2, row_at, k), row_pick, preferred_element_type=F32).astype(BF)
        col_all[k] = jnp.dot(bins(1, 3, lane, k), col_pick, preferred_element_type=F32).astype(BF)

    def build(i, half):
        at = half * HALF
        for j in range(POOL):
            weights[j * ROIS:(j + 1) * ROIS, at:at + HALF] = col_all[j, :, at:at + HALF] * row_all[i, :, at:at + HALF]
        return weights[:, at:at + HALF]

    def near_part(i, _):
        value = jnp.dot(build(i, 0), feat[0:HALF], preferred_element_type=F32)
        for k in range(2):
            s_flat[pl.ds(pl.multiple_of((k * POOL + i) * BINS, BINS), BINS)] = value[:, k * 128:(k + 1) * 128]
        return 0

    lax.fori_loop(0, POOL, near_part, 0)
    features.wait_recv()
    for row in range(ROWS):
        at = HALF + row * PITCH
        feat[at:at + COLS] = far[row]
    load_hw.wait()
    hid_acc[...] = jnp.zeros((ROIS, CHANNELS), F32)

    def share(i):
        return pltpu.make_async_remote_copy(
            src_ref=pooled.at[i, 0:ROIS], dst_ref=pooled.at[i, ROIS:2 * ROIS],
            send_sem=p_ss.at[i], recv_sem=p_rs.at[i], device_id=at_c, device_id_type=MESH,
        )

    def far_part(i, _):
        value = jnp.dot(build(i, 1), feat[HALF:2 * HALF], preferred_element_type=F32)
        near = [s_flat[pl.ds(pl.multiple_of((k * POOL + i) * BINS, BINS), BINS)] for k in range(2)]
        value = (value + jnp.concatenate(near, axis=1)).astype(BF)
        for j in range(POOL):
            pooled[i, 0:ROIS, j * CHANNELS:(j + 1) * CHANNELS] = value[j * ROIS:(j + 1) * ROIS]
        share(i).start()
        hid_acc[...] += jnp.dot(
            pooled[i, 0:ROIS], hw_ref[pl.ds(pl.multiple_of(i * WIDE, WIDE), WIDE)], preferred_element_type=F32
        )
        return 0

    lax.fori_loop(0, POOL, far_part, 0)

    pre_hidden = hid_acc[...]
    hidden = gelu_of(pre_hidden).astype(BF)
    part = jnp.dot(hidden, ow_ref[...], preferred_element_type=F32)
    z_s[...] = part.astype(BF)
    swap_z = one(z_s, z_r, m_ss.at[0], m_rs.at[0], at_s)
    hid_pair[0:ROIS] = hidden
    send_hid = one(hid_pair.at[0:ROIS], hid_pair.at[ROIS:2 * ROIS], m_ss.at[1], m_rs.at[1], at_c)
    slope = gelu_slope(pre_hidden)
    swap_z.wait_recv()
    pre_output = part + z_r[...].astype(F32)
    delta = (up_ref[...].astype(F32) * gelu_slope(pre_output)).astype(BF)
    od_pair[0:ROIS] = jnp.where(c == 0, delta[:, 0:256], delta[:, 256:512])
    od_s[...] = jnp.where(c == 0, delta[:, 256:512], delta[:, 0:256])
    send_od = one(od_s, od_pair.at[ROIS:2 * ROIS], m_ss.at[2], m_rs.at[2], at_c)
    back = lax.dot_general(delta, ow_ref[...], NT, preferred_element_type=F32)
    hidden_delta = (back * slope).astype(BF)
    hd_own[...] = hidden_delta
    hd_pair[0:ROIS] = jnp.where(c == 0, hidden_delta[:, 0:128], hidden_delta[:, 128:256])
    hd_s[...] = jnp.where(c == 0, hidden_delta[:, 128:256], hidden_delta[:, 0:128])
    send_hd = one(hd_s, hd_pair.at[ROIS:2 * ROIS], m_ss.at[3], m_rs.at[3], at_c)

    def wait_share(i, _):
        share(i).wait_recv()
        return 0

    send_hid.wait_recv()
    send_od.wait_recv()
    second = lax.dot_general(hid_pair[...], od_pair[...], TN, preferred_element_type=F32)
    for u in range(2):
        chunks[u, :, :, 0:8, :] = second[:, u * 128:(u + 1) * 128].reshape(8, 4, 8, 128)
        chunks[u, :, :, 200:208, :] = jnp.zeros((8, 4, 8, 128), F32)
    lax.fori_loop(0, POOL, wait_share, 0)
    send_hd.wait_recv()

    def weight_part(i, _):
        s_flat[pl.ds(pl.multiple_of(i * WIDE, WIDE), WIDE)] = lax.dot_general(
            pooled[i], hd_pair[...], TN, preferred_element_type=F32
        )
        return 0

    lax.fori_loop(0, POOL, weight_part, 0)

    def regroup(k, _):
        chunks[k // 32, (k // 4) % 8, k % 4, 8:204, :] = s_flat[pl.ds(k * 196, 196)]
        return 0

    lax.fori_loop(0, 64, regroup, 0)

    def ring(size, pos, to, own, send, recv, ssem, rsem):
        chains = chains_of(size // 2)
        live = {}

        def slot(k, h):
            return sum(ch[2] for ch in chains[:k]) + h

        def go(k, h):
            u, way, hops = chains[k]
            if h > 0:
                live[k, h - 1].wait_recv()
            dest = (pos + way * (hops - h) + size) % size
            value = own(u, dest)
            if h > 0:
                value = value + recv[slot(k, h - 1)].astype(F32)
            at = slot(k, h)
            send[at] = value.astype(BF)
            live[k, h] = pltpu.make_async_remote_copy(
                src_ref=send.at[at], dst_ref=recv.at[at], send_sem=ssem.at[at], recv_sem=rsem.at[at],
                device_id=to(way), device_id_type=MESH,
            )
            live[k, h].start()
            copies.append(live[k, h])

        def total(u):
            value = own(u, pos)
            for k, (piece, _, hops) in enumerate(chains):
                if piece == u and hops > 0:
                    live[k, hops - 1].wait_recv()
                    value = value + recv[slot(k, hops - 1)].astype(F32)
            return value

        return go, total

    za_go, za_total = ring(8, z, at_z, lambda u, d: chunks[u, d, :, 0:96, :], za_s, za_r, za_ss, za_rs)
    yb_go, yb_total = ring(4, y, at_y, lambda u, d: chunks[u, :, d, 96:208, :], yb_s, yb_r, yb_ss, yb_rs)
    ya_go, ya_total = ring(4, y, at_y, lambda u, d: acc_a[u, d], ya_s, ya_r, ya_ss, ya_rs)
    zb_go, zb_total = ring(8, z, at_z, lambda u, d: acc_b[u, d], zb_s, zb_r, zb_ss, zb_rs)

    def back_part(half):
        at = half * HALF

        def body(i, _):
            if half == 1:
                g = lax.dot_general(
                    hw_ref[pl.ds(pl.multiple_of(i * WIDE, WIDE), WIDE)], hd_own[...], NT, preferred_element_type=F32
                ).astype(BF)
                for j in range(POOL):
                    grads[i, :, j * ROIS:(j + 1) * ROIS] = g[j * CHANNELS:(j + 1) * CHANNELS]
            map_acc[:, at:at + HALF] += jnp.dot(grads[i], build(i, half), preferred_element_type=F32)
            return 0

        return body

    def work(half, low, high):
        lax.fori_loop(low, high, back_part(half), 0)

    for k in (0, 1):
        za_go(k, 0)
    for k in (0, 1):
        yb_go(k, 0)
    for k in (2, 3):
        za_go(k, 0)
    for k in (2, 3):
        yb_go(k, 0)
    map_acc[...] = jnp.zeros((CHANNELS, 2 * HALF), F32)
    work(1, 0, 3)
    for k in (0, 1, 2, 3):
        za_go(k, 1)
    for k in (0, 1):
        yb_go(k, 1)
    work(1, 3, 7)
    map_s[...] = jnp.transpose(map_acc[:, HALF:2 * HALF]).astype(BF)
    swap_map = one(map_s, map_r, m_ss.at[4], m_rs.at[4], at_s)
    for k in (0, 1, 2, 3):
        za_go(k, 2)
    work(0, 0, 3)
    for k in (0, 1):
        za_go(k, 3)
    for u in (0, 1):
        acc_b[u] = yb_total(u)
        zb_go(u, 0)
    for k in (2, 3):
        zb_go(k, 0)
    work(0, 3, 7)
    for u in (0, 1):
        acc_a[u] = za_total(u)
        ya_go(u, 0)
    for k in (2, 3):
        ya_go(k, 0)
    for k in (0, 1, 2, 3):
        zb_go(k, 1)
    for k in (0, 1):
        ya_go(k, 1)
    for k in (0, 1, 2, 3):
        zb_go(k, 2)
    near = jnp.transpose(map_acc[:, 0:HALF])
    for u in (0, 1):
        mid_a[u] = ya_total(u)
    for k in (0, 1):
        zb_go(k, 3)
    swap_map.wait_recv()
    whole = near + map_r[...].astype(F32)
    for row in range(ROWS):
        map_ref[row] = whole[row * PITCH:row * PITCH + COLS]
    for u in (0, 1):
        mid_b[u] = zb_total(u)

    x_s[0:96] = mid_a[1 - x].astype(BF)
    x_s[96:208] = mid_b[1 - x].astype(BF)
    across = one(x_s, x_r, xc_ss.at[0], xc_rs.at[0], at_x)
    across.wait_recv()
    final[0:96] = mid_a[x] + x_r[0:96].astype(F32)
    final[96:208] = mid_b[x] + x_r[96:208].astype(F32)

    gather[c, x, z, y] = final[0:8]
    mine = gather.at[c, x, z, y]
    steps = [one(mine, mine, g_ss.at[k], g_rs.at[k], at_z(k)) for k in range(1, 8)]
    low, high = final[8:106], final[106:204]
    c_s[...] = jnp.where(c == 0, high, low)
    swap = one(c_s, c_r, xc_ss.at[1], xc_rs.at[1], at_c)
    swap.wait_recv()
    kept = jnp.where(c == 0, low, high)
    got = c_r[...]
    first_ref[:, 0:128] = jnp.where(c == 0, kept, got)
    first_ref[:, 128:256] = jnp.where(c == 0, got, kept)
    for step in steps:
        step.wait_recv()
    steps = []
    for k in range(1, 4):
        column = gather.at[c, x, :, y]
        steps.append(one(column, column, g_ss.at[7 + k], g_rs.at[7 + k], at_y(k)))
    for step in steps:
        step.wait_recv()
    plane = gather.at[c, x]
    one(plane, plane, g_ss.at[11], g_rs.at[11], at_x).wait_recv()
    half = gather.at[c]
    one(half, half, g_ss.at[12], g_rs.at[12], at_c).wait_recv()
    for k in range(2):
        for u in range(2):
            at = k * 256 + u * 128
            second_ref[:, at:at + 128] = gather[k, u].reshape(256, 128)
    for copy in copies:
        copy.wait_send()

    def sent(i, _):
        share(i).wait_send()
        return 0

    lax.fori_loop(0, POOL, sent, 0)


def on_device(feature_map, proposals, hidden_weight, output_weight, upstream):
    dma = pltpu.SemaphoreType.DMA
    vmem = pl.BlockSpec(memory_space=pltpu.VMEM)
    first, second, grad = pl.pallas_call(
        step_kernel,
        out_shape=(
            jax.ShapeDtypeStruct((98, 256), F32),
            jax.ShapeDtypeStruct((256, 512), F32),
            jax.ShapeDtypeStruct((ROWS, COLS, CHANNELS), F32),
        ),
        in_specs=[vmem, vmem, pl.BlockSpec(memory_space=pl.ANY), vmem, vmem],
        out_specs=[vmem] * 3,
        scratch_shapes=[
            pltpu.VMEM((POOL * WIDE, 256), BF),
            pltpu.VMEM((2 * HALF, CHANNELS), BF),
            pltpu.VMEM((ROWS, COLS, CHANNELS), BF),
            pltpu.VMEM((POOL, ROIS, 2 * HALF), BF),
            pltpu.VMEM((POOL, ROIS, 2 * HALF), BF),
            pltpu.VMEM((BINS, 2 * HALF), BF),
            pltpu.VMEM((POOL, 2 * ROIS, WIDE), BF),
            pltpu.VMEM((ROIS, CHANNELS), F32),
            pltpu.VMEM((ROIS, 512), BF), pltpu.VMEM((ROIS, 512), BF),
            pltpu.VMEM((ROIS, 256), BF),
            pltpu.VMEM((2 * ROIS, 128), BF), pltpu.VMEM((ROIS, 128), BF),
            pltpu.VMEM((2 * ROIS, 256), BF), pltpu.VMEM((ROIS, 256), BF),
            pltpu.VMEM((2 * ROIS, 256), BF),
            pltpu.VMEM((POOL * WIDE, 128), F32),
            pltpu.VMEM((2, 8, 4, 208, 128), F32),
            pltpu.VMEM((POOL, CHANNELS, BINS), BF),
            pltpu.VMEM((CHANNELS, 2 * HALF), F32),
            pltpu.VMEM((HALF, CHANNELS), BF), pltpu.VMEM((HALF, CHANNELS), BF),
            pltpu.VMEM((14, 4, 96, 128), BF), pltpu.VMEM((14, 4, 96, 128), BF),
            pltpu.VMEM((6, 8, 112, 128), BF), pltpu.VMEM((6, 8, 112, 128), BF),
            pltpu.VMEM((6, 96, 128), BF), pltpu.VMEM((6, 96, 128), BF),
            pltpu.VMEM((14, 112, 128), BF), pltpu.VMEM((14, 112, 128), BF),
            pltpu.VMEM((208, 128), BF), pltpu.VMEM((208, 128), BF),
            pltpu.VMEM((98, 128), F32), pltpu.VMEM((98, 128), F32),
            pltpu.VMEM((2, 2, 8, 4, 8, 128), F32),
            pltpu.VMEM((2, 4, 96, 128), F32), pltpu.VMEM((2, 8, 112, 128), F32),
            pltpu.VMEM((2, 96, 128), F32), pltpu.VMEM((2, 112, 128), F32),
            pltpu.VMEM((208, 128), F32),
            dma(()), dma((2,)), dma((POOL,)), dma((POOL,)), dma((5,)), dma((5,)),
            dma((14,)), dma((14,)), dma((6,)), dma((6,)), dma((6,)), dma((6,)), dma((14,)), dma((14,)),
            dma((2,)), dma((2,)), dma((13,)), dma((13,)),
        ],
        compiler_params=pltpu.CompilerParams(
            collective_id=1, has_side_effects=True, vmem_limit_bytes=67043328
        ),
        name="box_head_step",
    )(feature_map[0], proposals[0], hidden_weight, output_weight, upstream[0])
    return (first, second, grad[None])


def solution(mesh):
    placed = (
        P("dp", "space", None, None),
        P("dp", None, None),
        P(None, "space"),
        P("space", None),
        P("dp", None, None),
    )
    return jax.shard_map(
        on_device,
        mesh=mesh,
        in_specs=placed,
        out_specs=(P("dp", "space"), P("space", None), P("dp", "space", None, None)),
        check_vma=False,
    )
```

```python
import jax
import jax.numpy as jnp
from jax import lax
from jax.experimental import pallas as pl
from jax.experimental.pallas import tpu as pltpu
from jax.sharding import PartitionSpec as P

MESH = pl.DeviceIdType.MESH
POOL = 7
ROIS = 128
CHANNELS = 256
ROWS = 12
COLS = 84
PITCH = 96
HALF = ROWS * PITCH
BINS = POOL * ROIS
WIDE = POOL * CHANNELS
BF = jnp.bfloat16
F32 = jnp.float32
TN = (((0,), (0,)), ((), ()))
NT = (((1,), (1,)), ((), ()))
SCALE = 0.7978845608028654
CUBIC = 0.044715


def gelu_of(v):
    return 0.5 * v * (1.0 + jnp.tanh(SCALE * (v + CUBIC * v * v * v)))


def gelu_slope(v):
    t = jnp.tanh(SCALE * (v + CUBIC * v * v * v))
    return 0.5 * (1.0 + t) + 0.5 * v * (1.0 - t * t) * (SCALE * (1.0 + 3.0 * CUBIC * v * v))


def place():
    me = lax.axis_index("dp")
    return me // 64, (me // 8) % 8, (me // 2) % 4, me % 2


def index_of(x, z, y, c):
    return ((x * 8 + z) * 4 + y) * 2 + c


def chains_of(hops):
    return ((0, 1, hops), (1, -1, hops), (0, -1, hops - 1), (1, 1, hops - 1))


def step_kernel(
    fm_ref, corner_ref, hw_hbm, ow_ref, up_ref, first_ref, second_ref, map_ref,
    hw_ref, feat, far, row_all, col_all, weights, pooled, hid_acc,
    z_s, z_r, hd_own, hd_pair, hd_s, od_pair, od_s, hid_pair, s_flat, chunks, grads, map_acc, map_s, map_r,
    za_s, za_r, yb_s, yb_r, ya_s, ya_r, zb_s, zb_r, x_s, x_r, c_s, c_r, t_ref, t_s1, t_r1, t_mid, t_s2, t_r2, t_s3, t_r3, t_all, t_far,
    acc_a, acc_b, mid_a, mid_b, final,
    hw_sem, f_sem, p_ss, p_rs, m_ss, m_rs,
    za_ss, za_rs, yb_ss, yb_rs, ya_ss, ya_rs, zb_ss, zb_rs, xc_ss, xc_rs, t_ss, t_rs,
):
    x, z, y, c = place()
    s = lax.axis_index("space")

    def at_z(step):
        return {"dp": index_of(x, (z + step + 8) % 8, y, c)}

    def at_y(step):
        return {"dp": index_of(x, z, (y + step + 4) % 4, c)}

    at_x = {"dp": index_of(1 - x, z, y, c)}
    at_c = {"dp": index_of(x, z, y, 1 - c)}
    at_s = {"space": 1 - s}

    load_hw = pltpu.make_async_copy(hw_hbm, hw_ref, hw_sem)
    load_hw.start()
    barrier = pltpu.get_barrier_semaphore()
    peers = [at_s, at_c] + [at_z(k) for k in range(1, 8)] + [at_y(k) for k in range(1, 4)] + [at_x]
    for peer in peers:
        pl.semaphore_signal(barrier, inc=1, device_id=peer, device_id_type=MESH)
    pl.semaphore_wait(barrier, len(peers))

    copies = []

    def one(src, dst, ssem, rsem, peer):
        copy = pltpu.make_async_remote_copy(
            src_ref=src, dst_ref=dst, send_sem=ssem, recv_sem=rsem, device_id=peer, device_id_type=MESH
        )
        copy.start()
        copies.append(copy)
        return copy

    features = one(fm_ref, far, f_sem.at[0], f_sem.at[1], at_s)

    feat[...] = jnp.zeros((2 * HALF, CHANNELS), BF)
    for row in range(ROWS):
        feat[row * PITCH:row * PITCH + COLS] = fm_ref[row]
    lane = lax.broadcasted_iota(jnp.int32, (ROIS, 128), 1).astype(F32)
    base = (ROWS * s).astype(F32)
    row_at = jnp.where(lane < ROWS, lane + base, lane - base)
    spot = lax.broadcasted_iota(jnp.int32, (128, 2 * HALF), 1).astype(F32)
    slot_at = lax.broadcasted_iota(jnp.int32, (128, 2 * HALF), 0).astype(F32)
    row_of = jnp.floor((spot + 0.5) * (1.0 / PITCH))
    row_pick = (row_of == slot_at).astype(F32).astype(BF)
    col_pick = jnp.logical_and(spot - row_of * PITCH == slot_at, slot_at < COLS).astype(F32).astype(BF)

    edges = corner_ref[...].astype(F32)
    edges = jnp.transpose(jnp.concatenate([edges, edges], axis=0))

    def bins(low, high, grid, k):
        start = edges[:, low:low + 1]
        size = (edges[:, high:high + 1] - start) / POOL
        total = jnp.zeros((ROIS, 128), F32)
        for offset in (0.25, 0.75):
            point = start + (k + offset) * size - 0.5
            total = total + jnp.maximum(0.0, 1.0 - jnp.abs(point - grid))
        return (0.5 * total).astype(BF)

    for k in range(POOL):
        row_all[k] = jnp.dot(bins(0, 2, row_at, k), row_pick, preferred_element_type=F32).astype(BF)
        col_all[k] = jnp.dot(bins(1, 3, lane, k), col_pick, preferred_element_type=F32).astype(BF)

    def build(i, half):
        at = half * HALF
        for j in range(POOL):
            weights[j * ROIS:(j + 1) * ROIS, at:at + HALF] = col_all[j, :, at:at + HALF] * row_all[i, :, at:at + HALF]
        return weights[:, at:at + HALF]

    def near_part(i, _):
        value = jnp.dot(build(i, 0), feat[0:HALF], preferred_element_type=F32)
        for k in range(2):
            s_flat[pl.ds(pl.multiple_of((k * POOL + i) * BINS, BINS), BINS)] = value[:, k * 128:(k + 1) * 128]
        return 0

    lax.fori_loop(0, POOL, near_part, 0)
    features.wait_recv()
    for row in range(ROWS):
        at = HALF + row * PITCH
        feat[at:at + COLS] = far[row]
    load_hw.wait()
    hid_acc[...] = jnp.zeros((ROIS, CHANNELS), F32)

    def share(i):
        return pltpu.make_async_remote_copy(
            src_ref=pooled.at[i, 0:ROIS], dst_ref=pooled.at[i, ROIS:2 * ROIS],
            send_sem=p_ss.at[i], recv_sem=p_rs.at[i], device_id=at_c, device_id_type=MESH,
        )

    def far_part(i, _):
        value = jnp.dot(build(i, 1), feat[HALF:2 * HALF], preferred_element_type=F32)
        near = [s_flat[pl.ds(pl.multiple_of((k * POOL + i) * BINS, BINS), BINS)] for k in range(2)]
        value = (value + jnp.concatenate(near, axis=1)).astype(BF)
        for j in range(POOL):
            pooled[i, 0:ROIS, j * CHANNELS:(j + 1) * CHANNELS] = value[j * ROIS:(j + 1) * ROIS]
        share(i).start()
        hid_acc[...] += jnp.dot(
            pooled[i, 0:ROIS], hw_ref[pl.ds(pl.multiple_of(i * WIDE, WIDE), WIDE)], preferred_element_type=F32
        )
        return 0

    lax.fori_loop(0, POOL, far_part, 0)

    pre_hidden = hid_acc[...]
    hidden = gelu_of(pre_hidden).astype(BF)
    part = jnp.dot(hidden, ow_ref[...], preferred_element_type=F32)
    z_s[...] = part.astype(BF)
    swap_z = one(z_s, z_r, m_ss.at[0], m_rs.at[0], at_s)
    hid_pair[0:ROIS] = hidden
    send_hid = one(hid_pair.at[0:ROIS], hid_pair.at[ROIS:2 * ROIS], m_ss.at[1], m_rs.at[1], at_c)
    slope = gelu_slope(pre_hidden)
    swap_z.wait_recv()
    pre_output = part + z_r[...].astype(F32)
    delta = (up_ref[...].astype(F32) * gelu_slope(pre_output)).astype(BF)
    od_pair[0:ROIS] = jnp.where(c == 0, delta[:, 0:256], delta[:, 256:512])
    od_s[...] = jnp.where(c == 0, delta[:, 256:512], delta[:, 0:256])
    send_od = one(od_s, od_pair.at[ROIS:2 * ROIS], m_ss.at[2], m_rs.at[2], at_c)
    back = lax.dot_general(delta, ow_ref[...], NT, preferred_element_type=F32)
    hidden_delta = (back * slope).astype(BF)
    hd_own[...] = hidden_delta
    hd_pair[0:ROIS] = jnp.where(c == 0, hidden_delta[:, 0:128], hidden_delta[:, 128:256])
    hd_s[...] = jnp.where(c == 0, hidden_delta[:, 128:256], hidden_delta[:, 0:128])
    send_hd = one(hd_s, hd_pair.at[ROIS:2 * ROIS], m_ss.at[3], m_rs.at[3], at_c)

    def wait_share(i, _):
        share(i).wait_recv()
        return 0

    send_hid.wait_recv()
    send_od.wait_recv()
    second = lax.dot_general(hid_pair[...], od_pair[...], TN, preferred_element_type=F32)
    chunks[:, :, :, 192:200, :] = jnp.zeros((2, 8, 4, 8, 128), F32)
    t_ref[...] = second.reshape(4, 8, 8, 256)
    t_s1[...] = t_ref[...].astype(BF)

    def to_rows():
        return [one(t_s1.at[(y + k) % 4], t_r1.at[k - 1], t_ss.at[k - 1], t_rs.at[k - 1], at_y(k)) for k in range(1, 4)]

    rows_moved = to_rows()
    lax.fori_loop(0, POOL, wait_share, 0)
    send_hd.wait_recv()

    def weight_part(i, _):
        s_flat[pl.ds(pl.multiple_of(i * WIDE, WIDE), WIDE)] = lax.dot_general(
            pooled[i], hd_pair[...], TN, preferred_element_type=F32
        )
        return 0

    lax.fori_loop(0, POOL, weight_part, 0)

    def regroup(k, _):
        chunks[k // 32, (k // 4) % 8, k % 4, 0:196, :] = s_flat[pl.ds(k * 196, 196)]
        return 0

    lax.fori_loop(0, 64, regroup, 0)

    def ring(size, pos, to, own, send, recv, ssem, rsem):
        chains = chains_of(size // 2)
        live = {}

        def slot(k, h):
            return sum(ch[2] for ch in chains[:k]) + h

        def go(k, h):
            u, way, hops = chains[k]
            if h > 0:
                live[k, h - 1].wait_recv()
            dest = (pos + way * (hops - h) + size) % size
            value = own(u, dest)
            if h > 0:
                value = value + recv[slot(k, h - 1)].astype(F32)
            at = slot(k, h)
            send[at] = value.astype(BF)
            live[k, h] = pltpu.make_async_remote_copy(
                src_ref=send.at[at], dst_ref=recv.at[at], send_sem=ssem.at[at], recv_sem=rsem.at[at],
                device_id=to(way), device_id_type=MESH,
            )
            live[k, h].start()
            copies.append(live[k, h])

        def total(u):
            value = own(u, pos)
            for k, (piece, _, hops) in enumerate(chains):
                if piece == u and hops > 0:
                    live[k, hops - 1].wait_recv()
                    value = value + recv[slot(k, hops - 1)].astype(F32)
            return value

        return go, total

    za_go, za_total = ring(8, z, at_z, lambda u, d: chunks[u, d, :, 0:112, :], za_s, za_r, za_ss, za_rs)
    yb_go, yb_total = ring(4, y, at_y, lambda u, d: chunks[u, :, d, 112:200, :], yb_s, yb_r, yb_ss, yb_rs)
    ya_go, ya_total = ring(4, y, at_y, lambda u, d: acc_a[u, d], ya_s, ya_r, ya_ss, ya_rs)
    zb_go, zb_total = ring(8, z, at_z, lambda u, d: acc_b[u, d], zb_s, zb_r, zb_ss, zb_rs)

    def take_rows():
        for copy in rows_moved:
            copy.wait_recv()
        t_mid[...] = t_ref[y] + (t_r1[0].astype(F32) + t_r1[1].astype(F32) + t_r1[2].astype(F32))
        t_s2[...] = t_mid[...].astype(BF)
        return [one(t_s2.at[(z + k) % 8], t_r2.at[k - 1], t_ss.at[k + 2], t_rs.at[k + 2], at_z(k)) for k in range(1, 8)]

    def take_cells(moved):
        for copy in moved:
            copy.wait_recv()
        total = t_mid[z]
        for k in range(7):
            total = total + t_r2[k].astype(F32)
        t_s3[...] = total.astype(BF)
        return one(t_s3, t_r3, t_ss.at[10], t_rs.at[10], at_x)

    def take_pair(moved):
        moved.wait_recv()
        t_all[y, z] = (t_s3[...].astype(F32) + t_r3[...].astype(F32)).astype(BF)
        mine = t_all.at[y, z]
        return [one(mine, mine, t_ss.at[10 + k], t_rs.at[10 + k], at_z(k)) for k in range(1, 8)]

    def spread_rows(moved):
        for copy in moved:
            copy.wait_recv()
        mine = t_all.at[y]
        return [one(mine, mine, t_ss.at[17 + k], t_rs.at[17 + k], at_y(k)) for k in range(1, 4)]

    def spread_core(moved):
        for copy in moved:
            copy.wait_recv()
        return one(t_all, t_far, t_ss.at[21], t_rs.at[21], at_c)

    def back_part(half):
        at = half * HALF

        def body(i, _):
            if half == 1:
                g = lax.dot_general(
                    hw_ref[pl.ds(pl.multiple_of(i * WIDE, WIDE), WIDE)], hd_own[...], NT, preferred_element_type=F32
                ).astype(BF)
                for j in range(POOL):
                    grads[i, :, j * ROIS:(j + 1) * ROIS] = g[j * CHANNELS:(j + 1) * CHANNELS]
            map_acc[:, at:at + HALF] += jnp.dot(grads[i], build(i, half), preferred_element_type=F32)
            return 0

        return body

    def work(half, low, high):
        lax.fori_loop(low, high, back_part(half), 0)

    for k in (0, 1):
        za_go(k, 0)
    for k in (0, 1):
        yb_go(k, 0)
    cells_moved = take_rows()
    for k in (2, 3):
        za_go(k, 0)
    for k in (2, 3):
        yb_go(k, 0)
    map_acc[...] = jnp.zeros((CHANNELS, 2 * HALF), F32)
    work(1, 0, 3)
    for k in (0, 1, 2, 3):
        za_go(k, 1)
    for k in (0, 1):
        yb_go(k, 1)
    pair_moved = take_cells(cells_moved)
    work(1, 3, 7)
    map_s[...] = jnp.transpose(map_acc[:, HALF:2 * HALF]).astype(BF)
    swap_map = one(map_s, map_r, m_ss.at[4], m_rs.at[4], at_s)
    for k in (0, 1, 2, 3):
        za_go(k, 2)
    cell_moved = take_pair(pair_moved)
    for u in (0, 1):
        acc_b[u] = yb_total(u)
        zb_go(u, 0)
    for k in (2, 3):
        zb_go(k, 0)
    work(0, 0, 3)
    for k in (0, 1):
        za_go(k, 3)
    for k in (0, 1, 2, 3):
        zb_go(k, 1)
    row_moved = spread_rows(cell_moved)
    work(0, 3, 7)
    for k in (0, 1, 2, 3):
        zb_go(k, 2)
    for u in (0, 1):
        acc_a[u] = za_total(u)
        ya_go(u, 0)
    for k in (2, 3):
        ya_go(k, 0)
    for k in (0, 1):
        zb_go(k, 3)
    core_moved = spread_core(row_moved)
    near = jnp.transpose(map_acc[:, 0:HALF])
    for k in (0, 1):
        ya_go(k, 1)
    swap_map.wait_recv()
    whole = near + map_r[...].astype(F32)
    for row in range(ROWS):
        for k in range(2):
            map_ref[pl.ds(row * 2 * COLS + k, COLS, stride=2), :] = whole[
                row * PITCH:row * PITCH + COLS, k * 128:(k + 1) * 128
            ]
    for u in (0, 1):
        mid_b[u] = zb_total(u)
    for u in (0, 1):
        mid_a[u] = ya_total(u)

    x_s[0:112] = mid_a[1 - x].astype(BF)
    x_s[112:200] = mid_b[1 - x].astype(BF)
    across = one(x_s, x_r, xc_ss.at[0], xc_rs.at[0], at_x)
    across.wait_recv()
    final[0:112] = mid_a[x] + x_r[0:112].astype(F32)
    final[112:200] = mid_b[x] + x_r[112:200].astype(F32)

    low, high = final[0:98], final[98:196]
    c_s[...] = jnp.where(c == 0, high, low)
    swap = one(c_s, c_r, xc_ss.at[1], xc_rs.at[1], at_c)
    swap.wait_recv()
    kept = jnp.where(c == 0, low, high)
    got = c_r[...]
    first_ref[:, 0:128] = jnp.where(c == 0, kept, got)
    first_ref[:, 128:256] = jnp.where(c == 0, got, kept)
    core_moved.wait_recv()
    here = t_all[...].astype(F32).reshape(256, 256)
    there = t_far[...].astype(F32).reshape(256, 256)
    second_ref[:, 0:256] = jnp.where(c == 0, here, there)
    second_ref[:, 256:512] = jnp.where(c == 0, there, here)
    for copy in copies:
        copy.wait_send()

    def sent(i, _):
        share(i).wait_send()
        return 0

    lax.fori_loop(0, POOL, sent, 0)


def hand_over(first_ref, second_ref, map_ref, first_out, second_out, map_out):
    first_out[...] = first_ref[...]
    second_out[...] = second_ref[...]
    map_out[...] = map_ref[...]


def on_device(feature_map, proposals, hidden_weight, output_weight, upstream):
    dma = pltpu.SemaphoreType.DMA
    vmem = pl.BlockSpec(memory_space=pltpu.VMEM)
    first, second, grad = pl.pallas_call(
        step_kernel,
        out_shape=(
            jax.ShapeDtypeStruct((98, 256), F32),
            jax.ShapeDtypeStruct((256, 512), F32),
            jax.ShapeDtypeStruct((2 * ROWS * COLS, 128), F32),
        ),
        in_specs=[vmem, vmem, pl.BlockSpec(memory_space=pl.ANY), vmem, vmem],
        out_specs=[vmem] * 3,
        scratch_shapes=[
            pltpu.VMEM((POOL * WIDE, 256), BF),
            pltpu.VMEM((2 * HALF, CHANNELS), BF),
            pltpu.VMEM((ROWS, COLS, CHANNELS), BF),
            pltpu.VMEM((POOL, ROIS, 2 * HALF), BF),
            pltpu.VMEM((POOL, ROIS, 2 * HALF), BF),
            pltpu.VMEM((BINS, 2 * HALF), BF),
            pltpu.VMEM((POOL, 2 * ROIS, WIDE), BF),
            pltpu.VMEM((ROIS, CHANNELS), F32),
            pltpu.VMEM((ROIS, 512), BF), pltpu.VMEM((ROIS, 512), BF),
            pltpu.VMEM((ROIS, 256), BF),
            pltpu.VMEM((2 * ROIS, 128), BF), pltpu.VMEM((ROIS, 128), BF),
            pltpu.VMEM((2 * ROIS, 256), BF), pltpu.VMEM((ROIS, 256), BF),
            pltpu.VMEM((2 * ROIS, 256), BF),
            pltpu.VMEM((POOL * WIDE, 128), F32),
            pltpu.VMEM((2, 8, 4, 200, 128), F32),
            pltpu.VMEM((POOL, CHANNELS, BINS), BF),
            pltpu.VMEM((CHANNELS, 2 * HALF), F32),
            pltpu.VMEM((HALF, CHANNELS), BF), pltpu.VMEM((HALF, CHANNELS), BF),
            pltpu.VMEM((14, 4, 112, 128), BF), pltpu.VMEM((14, 4, 112, 128), BF),
            pltpu.VMEM((6, 8, 88, 128), BF), pltpu.VMEM((6, 8, 88, 128), BF),
            pltpu.VMEM((6, 112, 128), BF), pltpu.VMEM((6, 112, 128), BF),
            pltpu.VMEM((14, 88, 128), BF), pltpu.VMEM((14, 88, 128), BF),
            pltpu.VMEM((200, 128), BF), pltpu.VMEM((200, 128), BF),
            pltpu.VMEM((98, 128), F32), pltpu.VMEM((98, 128), F32),
            pltpu.VMEM((4, 8, 8, 256), F32), pltpu.VMEM((4, 8, 8, 256), BF), pltpu.VMEM((3, 8, 8, 256), BF),
            pltpu.VMEM((8, 8, 256), F32), pltpu.VMEM((8, 8, 256), BF), pltpu.VMEM((7, 8, 256), BF),
            pltpu.VMEM((8, 256), BF), pltpu.VMEM((8, 256), BF),
            pltpu.VMEM((4, 8, 8, 256), BF), pltpu.VMEM((4, 8, 8, 256), BF),
            pltpu.VMEM((2, 4, 112, 128), F32), pltpu.VMEM((2, 8, 88, 128), F32),
            pltpu.VMEM((2, 112, 128), F32), pltpu.VMEM((2, 88, 128), F32),
            pltpu.VMEM((200, 128), F32),
            dma(()), dma((2,)), dma((POOL,)), dma((POOL,)), dma((5,)), dma((5,)),
            dma((14,)), dma((14,)), dma((6,)), dma((6,)), dma((6,)), dma((6,)), dma((14,)), dma((14,)),
            dma((2,)), dma((2,)), dma((22,)), dma((22,)),
        ],
        compiler_params=pltpu.CompilerParams(
            collective_id=1, has_side_effects=True, vmem_limit_bytes=67043328
        ),
        name="box_head_step",
    )(feature_map[0], jnp.transpose(proposals[0]), hidden_weight, output_weight, upstream[0])
    first, second, grad = pl.pallas_call(
        hand_over,
        out_shape=tuple(jax.ShapeDtypeStruct(v.shape, v.dtype) for v in (first, second, grad)),
        in_specs=[vmem] * 3,
        out_specs=[vmem] * 3,
        name="hand_over",
    )(first, second, grad)
    return (first, second, grad.reshape(1, ROWS, COLS, CHANNELS))


def solution(mesh):
    placed = (
        P("dp", "space", None, None),
        P("dp", None, None),
        P(None, "space"),
        P("space", None),
        P("dp", None, None),
    )
    return jax.shard_map(
        on_device,
        mesh=mesh,
        in_specs=placed,
        out_specs=(P("dp", "space"), P("space", None), P("dp", "space", None, None)),
        check_vma=False,
    )
```

```python
import jax
import jax.numpy as jnp
from jax import lax
from jax.experimental import pallas as pl
from jax.experimental.pallas import tpu as pltpu
from jax.sharding import PartitionSpec as P

MESH = pl.DeviceIdType.MESH
POOL = 7
ROIS = 128
CHANNELS = 256
ROWS = 12
COLS = 84
CELLS = ROWS * COLS
HALF = 1024
FIRST = 768
BINS = POOL * ROIS
WIDE = POOL * CHANNELS
BF = jnp.bfloat16
F32 = jnp.float32
TN = (((0,), (0,)), ((), ()))
NT = (((1,), (1,)), ((), ()))
SCALE = 0.7978845608028654
CUBIC = 0.044715


def gelu_of(v):
    return 0.5 * v * (1.0 + jnp.tanh(SCALE * (v + CUBIC * v * v * v)))


def gelu_slope(v):
    t = jnp.tanh(SCALE * (v + CUBIC * v * v * v))
    return 0.5 * (1.0 + t) + 0.5 * v * (1.0 - t * t) * (SCALE * (1.0 + 3.0 * CUBIC * v * v))


def place():
    me = lax.axis_index("dp")
    return me // 64, (me // 8) % 8, (me // 2) % 4, me % 2


def index_of(x, z, y, c):
    return ((x * 8 + z) * 4 + y) * 2 + c


def chains_of(hops):
    return ((0, 1, hops), (1, -1, hops), (0, -1, hops - 1), (1, 1, hops - 1))


def step_kernel(
    fm_ref, corner_ref, hw_hbm, ow_ref, up_ref, first_ref, second_ref, map_ref,
    hw_ref, feat, flat, row_all, col_all, weights, pooled, hid_acc,
    z_s, z_r, hd_own, hd_pair, hd_s, od_pair, od_s, hid_pair, s_flat, chunks, grads, map_acc, map_s, map_r,
    za_s, za_r, yb_s, yb_r, ya_s, ya_r, zb_s, zb_r, x_s, x_r, c_s, c_r, t_ref, t_s1, t_r1, t_mid, t_s2, t_r2, t_s3, t_r3, t_all, t_far,
    acc_a, acc_b, mid_a, mid_b, final,
    hw_sem, f_sem, p_ss, p_rs, m_ss, m_rs,
    za_ss, za_rs, yb_ss, yb_rs, ya_ss, ya_rs, zb_ss, zb_rs, xc_ss, xc_rs, t_ss, t_rs,
):
    x, z, y, c = place()
    s = lax.axis_index("space")

    def at_z(step):
        return {"dp": index_of(x, (z + step + 8) % 8, y, c)}

    def at_y(step):
        return {"dp": index_of(x, z, (y + step + 4) % 4, c)}

    at_x = {"dp": index_of(1 - x, z, y, c)}
    at_c = {"dp": index_of(x, z, y, 1 - c)}
    at_s = {"space": 1 - s}

    load_hw = pltpu.make_async_copy(hw_hbm, hw_ref, hw_sem)
    load_hw.start()
    barrier = pltpu.get_barrier_semaphore()
    peers = [at_s, at_c] + [at_z(k) for k in range(1, 8)] + [at_y(k) for k in range(1, 4)] + [at_x]
    for peer in peers:
        pl.semaphore_signal(barrier, inc=1, device_id=peer, device_id_type=MESH)

    copies = []

    def one(src, dst, ssem, rsem, peer):
        copy = pltpu.make_async_remote_copy(
            src_ref=src, dst_ref=dst, send_sem=ssem, recv_sem=rsem, device_id=peer, device_id_type=MESH
        )
        copy.start()
        copies.append(copy)
        return copy

    flat[CELLS:HALF] = jnp.zeros((HALF - CELLS, CHANNELS), F32)
    for row in range(ROWS):
        flat[row * COLS:(row + 1) * COLS] = fm_ref[row].astype(F32)
    feat[0:HALF] = flat[...].astype(BF)
    lane = lax.broadcasted_iota(jnp.int32, (ROIS, 128), 1).astype(F32)
    base = (ROWS * s).astype(F32)
    row_at = jnp.where(lane < ROWS, lane + base, lane - base)
    spot = lax.broadcasted_iota(jnp.int32, (128, HALF), 1).astype(F32)
    slot_at = lax.broadcasted_iota(jnp.int32, (128, HALF), 0).astype(F32)
    row_of = jnp.floor((spot + 0.5) * (1.0 / COLS))
    inside = spot < CELLS
    row_pick = [
        jnp.logical_and(row_of + first == slot_at, inside).astype(F32).astype(BF) for first in (0, ROWS)
    ]
    col_pick = jnp.logical_and(spot - row_of * COLS == slot_at, inside).astype(F32).astype(BF)

    edges = corner_ref[...].astype(F32)
    edges = jnp.transpose(jnp.concatenate([edges, edges], axis=0))

    def bins(low, high, grid, k):
        start = edges[:, low:low + 1]
        size = (edges[:, high:high + 1] - start) / POOL
        total = jnp.zeros((ROIS, 128), F32)
        for offset in (0.25, 0.75):
            point = start + (k + offset) * size - 0.5
            total = total + jnp.maximum(0.0, 1.0 - jnp.abs(point - grid))
        return (0.5 * total).astype(BF)

    for k in range(POOL):
        rows = bins(0, 2, row_at, k)
        for half in range(2):
            row_all[k, :, half * HALF:(half + 1) * HALF] = jnp.dot(
                rows, row_pick[half], preferred_element_type=F32
            ).astype(BF)
        col_all[k] = jnp.dot(bins(1, 3, lane, k), col_pick, preferred_element_type=F32).astype(BF)

    pl.semaphore_wait(barrier, len(peers))
    features = [
        one(feat.at[low:high], feat.at[HALF + low:HALF + high], f_sem.at[k], f_sem.at[2 + k], at_s)
        for k, (low, high) in enumerate(((0, FIRST), (FIRST, HALF)))
    ]

    def build(i, half, low=0, high=HALF):
        at = half * HALF
        for j in range(POOL):
            weights[j * ROIS:(j + 1) * ROIS, low:high] = (
                col_all[j, :, low:high] * row_all[i, :, at + low:at + high]
            )
        return weights[:, low:high]

    def held(i, k):
        return pl.ds(pl.multiple_of((k * POOL + i) * BINS, BINS), BINS)

    def near_part(i, _):
        value = jnp.dot(build(i, 0), feat[0:HALF], preferred_element_type=F32)
        for k in range(2):
            s_flat[held(i, k)] = value[:, k * 128:(k + 1) * 128]
        return 0

    def far_first(i, _):
        value = jnp.dot(build(i, 1, 0, FIRST), feat[HALF:HALF + FIRST], preferred_element_type=F32)
        for k in range(2):
            s_flat[held(i, k)] += value[:, k * 128:(k + 1) * 128]
        return 0

    lax.fori_loop(0, POOL, near_part, 0)
    features[0].wait_recv()
    lax.fori_loop(0, POOL, far_first, 0)
    features[1].wait_recv()
    load_hw.wait()
    hid_acc[...] = jnp.zeros((ROIS, CHANNELS), F32)

    def share(i):
        return pltpu.make_async_remote_copy(
            src_ref=pooled.at[i, 0:ROIS], dst_ref=pooled.at[i, ROIS:2 * ROIS],
            send_sem=p_ss.at[i], recv_sem=p_rs.at[i], device_id=at_c, device_id_type=MESH,
        )

    def far_part(i, _):
        value = jnp.dot(build(i, 1, FIRST, HALF), feat[HALF + FIRST:2 * HALF], preferred_element_type=F32)
        near = [s_flat[held(i, k)] for k in range(2)]
        value = (value + jnp.concatenate(near, axis=1)).astype(BF)
        for j in range(POOL):
            pooled[i, 0:ROIS, j * CHANNELS:(j + 1) * CHANNELS] = value[j * ROIS:(j + 1) * ROIS]
        share(i).start()
        hid_acc[...] += jnp.dot(
            pooled[i, 0:ROIS], hw_ref[pl.ds(pl.multiple_of(i * WIDE, WIDE), WIDE)], preferred_element_type=F32
        )
        return 0

    lax.fori_loop(0, POOL, far_part, 0)

    pre_hidden = hid_acc[...]
    hidden = gelu_of(pre_hidden).astype(BF)
    part = jnp.dot(hidden, ow_ref[...], preferred_element_type=F32)
    z_s[...] = part.astype(BF)
    swap_z = one(z_s, z_r, m_ss.at[0], m_rs.at[0], at_s)
    hid_pair[0:ROIS] = hidden
    send_hid = one(hid_pair.at[0:ROIS], hid_pair.at[ROIS:2 * ROIS], m_ss.at[1], m_rs.at[1], at_c)
    slope = gelu_slope(pre_hidden)
    swap_z.wait_recv()
    pre_output = part + z_r[...].astype(F32)
    delta = (up_ref[...].astype(F32) * gelu_slope(pre_output)).astype(BF)
    od_pair[0:ROIS] = jnp.where(c == 0, delta[:, 0:256], delta[:, 256:512])
    od_s[...] = jnp.where(c == 0, delta[:, 256:512], delta[:, 0:256])
    send_od = one(od_s, od_pair.at[ROIS:2 * ROIS], m_ss.at[2], m_rs.at[2], at_c)
    back = lax.dot_general(delta, ow_ref[...], NT, preferred_element_type=F32)
    hidden_delta = (back * slope).astype(BF)
    hd_own[...] = hidden_delta
    hd_pair[0:ROIS] = jnp.where(c == 0, hidden_delta[:, 0:128], hidden_delta[:, 128:256])
    hd_s[...] = jnp.where(c == 0, hidden_delta[:, 128:256], hidden_delta[:, 0:128])
    send_hd = one(hd_s, hd_pair.at[ROIS:2 * ROIS], m_ss.at[3], m_rs.at[3], at_c)

    def wait_share(i, _):
        share(i).wait_recv()
        return 0

    send_hid.wait_recv()
    send_od.wait_recv()
    second = lax.dot_general(hid_pair[...], od_pair[...], TN, preferred_element_type=F32)
    t_ref[...] = second.reshape(4, 8, 8, 256)
    t_s1[...] = t_ref[...].astype(BF)

    def to_rows():
        return [one(t_s1.at[(y + k) % 4], t_r1.at[k - 1], t_ss.at[k - 1], t_rs.at[k - 1], at_y(k)) for k in range(1, 4)]

    rows_moved = to_rows()
    lax.fori_loop(0, POOL, wait_share, 0)
    send_hd.wait_recv()

    def weight_part(i, _):
        s_flat[pl.ds(pl.multiple_of(i * WIDE, WIDE), WIDE)] = lax.dot_general(
            pooled[i], hd_pair[...], TN, preferred_element_type=F32
        )
        return 0

    lax.fori_loop(0, POOL, weight_part, 0)

    def regroup(k, _):
        value = jnp.concatenate([s_flat[pl.ds(k * 196, 196)], jnp.zeros((4, 128), F32)], axis=0)
        chunks[k // 32, (k // 4) % 8, k % 4] = value.astype(BF)
        return 0

    lax.fori_loop(0, 64, regroup, 0)

    def ring(size, pos, to, own, send, recv, ssem, rsem):
        chains = chains_of(size // 2)
        live = {}

        def slot(k, h):
            return sum(ch[2] for ch in chains[:k]) + h

        def go(k, h):
            u, way, hops = chains[k]
            at = slot(k, h)
            source = own(u, (pos + way * (hops - h) + size) % size)
            if h > 0:
                live[k, h - 1].wait_recv()
                send[at] = source[...] + recv[at - 1]
                source = send.at[at]
            live[k, h] = one(source, recv.at[at], ssem.at[at], rsem.at[at], to(way))

        def total(u):
            value = own(u, pos)[...].astype(F32)
            for k, (piece, _, hops) in enumerate(chains):
                if piece == u and hops > 0:
                    live[k, hops - 1].wait_recv()
                    value = value + recv[slot(k, hops - 1)].astype(F32)
            return value

        return go, total

    za_go, za_total = ring(8, z, at_z, lambda u, d: chunks.at[u, d, :, 0:112, :], za_s, za_r, za_ss, za_rs)
    yb_go, yb_total = ring(4, y, at_y, lambda u, d: chunks.at[u, :, d, 112:200, :], yb_s, yb_r, yb_ss, yb_rs)
    ya_go, ya_total = ring(4, y, at_y, lambda u, d: acc_a.at[u, d], ya_s, ya_r, ya_ss, ya_rs)
    zb_go, zb_total = ring(8, z, at_z, lambda u, d: acc_b.at[u, d], zb_s, zb_r, zb_ss, zb_rs)

    def take_rows():
        for copy in rows_moved:
            copy.wait_recv()
        t_mid[...] = t_ref[y] + (t_r1[0].astype(F32) + t_r1[1].astype(F32) + t_r1[2].astype(F32))
        t_s2[...] = t_mid[...].astype(BF)
        return [one(t_s2.at[(z + k) % 8], t_r2.at[k - 1], t_ss.at[k + 2], t_rs.at[k + 2], at_z(k)) for k in range(1, 8)]

    def take_cells(moved):
        for copy in moved:
            copy.wait_recv()
        total = t_mid[z]
        for k in range(7):
            total = total + t_r2[k].astype(F32)
        t_s3[...] = total.astype(BF)
        return one(t_s3, t_r3, t_ss.at[10], t_rs.at[10], at_x)

    def take_pair(moved):
        moved.wait_recv()
        t_all[y, z] = (t_s3[...].astype(F32) + t_r3[...].astype(F32)).astype(BF)
        mine = t_all.at[y, z]
        return [one(mine, mine, t_ss.at[10 + k], t_rs.at[10 + k], at_z(k)) for k in range(1, 8)]

    def spread_rows(moved):
        for copy in moved:
            copy.wait_recv()
        mine = t_all.at[y]
        return [one(mine, mine, t_ss.at[17 + k], t_rs.at[17 + k], at_y(k)) for k in range(1, 4)]

    def spread_core(moved):
        for copy in moved:
            copy.wait_recv()
        return one(t_all, t_far, t_ss.at[21], t_rs.at[21], at_c)

    def back_part(half):
        at = half * HALF

        def body(i, _):
            if half == 1:
                g = lax.dot_general(
                    hw_ref[pl.ds(pl.multiple_of(i * WIDE, WIDE), WIDE)], hd_own[...], NT, preferred_element_type=F32
                ).astype(BF)
                for j in range(POOL):
                    grads[i, :, j * ROIS:(j + 1) * ROIS] = g[j * CHANNELS:(j + 1) * CHANNELS]
            map_acc[:, at:at + HALF] += jnp.dot(grads[i], build(i, half), preferred_element_type=F32)
            return 0

        return body

    def work(half, low, high):
        lax.fori_loop(low, high, back_part(half), 0)

    for k in (0, 1):
        za_go(k, 0)
    for k in (0, 1):
        yb_go(k, 0)
    cells_moved = take_rows()
    for k in (2, 3):
        za_go(k, 0)
    for k in (2, 3):
        yb_go(k, 0)
    map_acc[...] = jnp.zeros((CHANNELS, 2 * HALF), F32)
    work(1, 0, 3)
    for k in (0, 1, 2, 3):
        za_go(k, 1)
    for k in (0, 1):
        yb_go(k, 1)
    pair_moved = take_cells(cells_moved)
    work(1, 3, 7)
    map_s[...] = jnp.transpose(map_acc[:, HALF:2 * HALF]).astype(BF)
    swap_map = one(map_s, map_r, m_ss.at[4], m_rs.at[4], at_s)
    for k in (0, 1, 2, 3):
        za_go(k, 2)
    cell_moved = take_pair(pair_moved)
    for u in (0, 1):
        acc_b[u] = yb_total(u).astype(BF)
        zb_go(u, 0)
    for k in (2, 3):
        zb_go(k, 0)
    work(0, 0, 3)
    for k in (0, 1):
        za_go(k, 3)
    for k in (0, 1, 2, 3):
        zb_go(k, 1)
    row_moved = spread_rows(cell_moved)
    work(0, 3, 7)
    for k in (0, 1, 2, 3):
        zb_go(k, 2)
    for u in (0, 1):
        acc_a[u] = za_total(u).astype(BF)
        ya_go(u, 0)
    for k in (2, 3):
        ya_go(k, 0)
    for k in (0, 1):
        zb_go(k, 3)
    core_moved = spread_core(row_moved)
    near = jnp.transpose(map_acc[:, 0:HALF])
    for k in (0, 1):
        ya_go(k, 1)
    swap_map.wait_recv()
    whole = near + map_r[...].astype(F32)
    for k in range(2):
        map_ref[pl.ds(k, CELLS, stride=2), :] = whole[0:CELLS, k * 128:(k + 1) * 128]
    for u in (0, 1):
        mid_b[u] = zb_total(u)
    for u in (0, 1):
        mid_a[u] = ya_total(u)

    x_s[0:112] = mid_a[1 - x].astype(BF)
    x_s[112:200] = mid_b[1 - x].astype(BF)
    across = one(x_s, x_r, xc_ss.at[0], xc_rs.at[0], at_x)
    across.wait_recv()
    final[0:112] = mid_a[x] + x_r[0:112].astype(F32)
    final[112:200] = mid_b[x] + x_r[112:200].astype(F32)

    low, high = final[0:98], final[98:196]
    c_s[...] = jnp.where(c == 0, high, low)
    swap = one(c_s, c_r, xc_ss.at[1], xc_rs.at[1], at_c)
    swap.wait_recv()
    kept = jnp.where(c == 0, low, high)
    got = c_r[...]
    first_ref[:, 0:128] = jnp.where(c == 0, kept, got)
    first_ref[:, 128:256] = jnp.where(c == 0, got, kept)
    core_moved.wait_recv()
    here = t_all[...].astype(F32).reshape(256, 256)
    there = t_far[...].astype(F32).reshape(256, 256)
    second_ref[:, 0:256] = jnp.where(c == 0, here, there)
    second_ref[:, 256:512] = jnp.where(c == 0, there, here)
    for copy in copies:
        copy.wait_send()

    def sent(i, _):
        share(i).wait_send()
        return 0

    lax.fori_loop(0, POOL, sent, 0)


def hand_over(first_ref, second_ref, map_ref, first_out, second_out, map_out):
    first_out[...] = first_ref[...]
    second_out[...] = second_ref[...]
    map_out[...] = map_ref[...]


def on_device(feature_map, proposals, hidden_weight, output_weight, upstream):
    dma = pltpu.SemaphoreType.DMA
    vmem = pl.BlockSpec(memory_space=pltpu.VMEM)
    first, second, grad = pl.pallas_call(
        step_kernel,
        out_shape=(
            jax.ShapeDtypeStruct((98, 256), F32),
            jax.ShapeDtypeStruct((256, 512), F32),
            jax.ShapeDtypeStruct((2 * ROWS * COLS, 128), F32),
        ),
        in_specs=[vmem, vmem, pl.BlockSpec(memory_space=pl.ANY), vmem, vmem],
        out_specs=[vmem] * 3,
        scratch_shapes=[
            pltpu.VMEM((POOL * WIDE, 256), BF),
            pltpu.VMEM((2 * HALF, CHANNELS), BF),
            pltpu.VMEM((HALF, CHANNELS), F32),
            pltpu.VMEM((POOL, ROIS, 2 * HALF), BF),
            pltpu.VMEM((POOL, ROIS, HALF), BF),
            pltpu.VMEM((BINS, HALF), BF),
            pltpu.VMEM((POOL, 2 * ROIS, WIDE), BF),
            pltpu.VMEM((ROIS, CHANNELS), F32),
            pltpu.VMEM((ROIS, 512), BF), pltpu.VMEM((ROIS, 512), BF),
            pltpu.VMEM((ROIS, 256), BF),
            pltpu.VMEM((2 * ROIS, 128), BF), pltpu.VMEM((ROIS, 128), BF),
            pltpu.VMEM((2 * ROIS, 256), BF), pltpu.VMEM((ROIS, 256), BF),
            pltpu.VMEM((2 * ROIS, 256), BF),
            pltpu.VMEM((POOL * WIDE, 128), F32),
            pltpu.VMEM((2, 8, 4, 200, 128), BF),
            pltpu.VMEM((POOL, CHANNELS, BINS), BF),
            pltpu.VMEM((CHANNELS, 2 * HALF), F32),
            pltpu.VMEM((HALF, CHANNELS), BF), pltpu.VMEM((HALF, CHANNELS), BF),
            pltpu.VMEM((14, 4, 112, 128), BF), pltpu.VMEM((14, 4, 112, 128), BF),
            pltpu.VMEM((6, 8, 88, 128), BF), pltpu.VMEM((6, 8, 88, 128), BF),
            pltpu.VMEM((6, 112, 128), BF), pltpu.VMEM((6, 112, 128), BF),
            pltpu.VMEM((14, 88, 128), BF), pltpu.VMEM((14, 88, 128), BF),
            pltpu.VMEM((200, 128), BF), pltpu.VMEM((200, 128), BF),
            pltpu.VMEM((98, 128), F32), pltpu.VMEM((98, 128), F32),
            pltpu.VMEM((4, 8, 8, 256), F32), pltpu.VMEM((4, 8, 8, 256), BF), pltpu.VMEM((3, 8, 8, 256), BF),
            pltpu.VMEM((8, 8, 256), F32), pltpu.VMEM((8, 8, 256), BF), pltpu.VMEM((7, 8, 256), BF),
            pltpu.VMEM((8, 256), BF), pltpu.VMEM((8, 256), BF),
            pltpu.VMEM((4, 8, 8, 256), BF), pltpu.VMEM((4, 8, 8, 256), BF),
            pltpu.VMEM((2, 4, 112, 128), BF), pltpu.VMEM((2, 8, 88, 128), BF),
            pltpu.VMEM((2, 112, 128), F32), pltpu.VMEM((2, 88, 128), F32),
            pltpu.VMEM((200, 128), F32),
            dma(()), dma((4,)), dma((POOL,)), dma((POOL,)), dma((5,)), dma((5,)),
            dma((14,)), dma((14,)), dma((6,)), dma((6,)), dma((6,)), dma((6,)), dma((14,)), dma((14,)),
            dma((2,)), dma((2,)), dma((22,)), dma((22,)),
        ],
        compiler_params=pltpu.CompilerParams(
            collective_id=1, has_side_effects=True, vmem_limit_bytes=67043328
        ),
        name="box_head_step",
    )(feature_map[0], jnp.transpose(proposals[0]), hidden_weight, output_weight, upstream[0])
    first, second, grad = pl.pallas_call(
        hand_over,
        out_shape=tuple(jax.ShapeDtypeStruct(v.shape, v.dtype) for v in (first, second, grad)),
        in_specs=[vmem] * 3,
        out_specs=[vmem] * 3,
        name="hand_over",
    )(first, second, grad)
    return (first, second, grad.reshape(1, ROWS, COLS, CHANNELS))


def solution(mesh):
    placed = (
        P("dp", "space", None, None),
        P("dp", None, None),
        P(None, "space"),
        P("space", None),
        P("dp", None, None),
    )
    return jax.shard_map(
        on_device,
        mesh=mesh,
        in_specs=placed,
        out_specs=(P("dp", "space"), P("space", None), P("dp", "space", None, None)),
        check_vma=False,
    )
```

```python
import jax
import jax.numpy as jnp
from jax import lax
from jax.experimental import pallas as pl
from jax.experimental.pallas import tpu as pltpu
from jax.sharding import PartitionSpec as P

MESH = pl.DeviceIdType.MESH
POOL = 7
ROIS = 128
CHANNELS = 256
ROWS = 12
COLS = 84
CELLS = ROWS * COLS
HALF = 1024
FIRST = 768
BINS = POOL * ROIS
WIDE = POOL * CHANNELS
BF = jnp.bfloat16
F32 = jnp.float32
TN = (((0,), (0,)), ((), ()))
NT = (((1,), (1,)), ((), ()))
SCALE = 0.7978845608028654
CUBIC = 0.044715


def gelu_of(v):
    return 0.5 * v * (1.0 + jnp.tanh(SCALE * (v + CUBIC * v * v * v)))


def gelu_slope(v):
    t = jnp.tanh(SCALE * (v + CUBIC * v * v * v))
    return 0.5 * (1.0 + t) + 0.5 * v * (1.0 - t * t) * (SCALE * (1.0 + 3.0 * CUBIC * v * v))


def place():
    me = lax.axis_index("dp")
    return me // 64, (me // 8) % 8, (me // 2) % 4, me % 2


def index_of(x, z, y, c):
    return ((x * 8 + z) * 4 + y) * 2 + c


def chains_of(hops):
    return ((0, 1, hops), (1, -1, hops), (0, -1, hops - 1), (1, 1, hops - 1))


def step_kernel(
    fm_ref, corner_ref, hw_hbm, ow_ref, up_ref, first_ref, second_ref, map_ref,
    hw_ref, feat, flat, row_all, col_all, weights, pooled, hid_acc,
    z_s, z_r, hd_own, hd_pair, hd_s, od_pair, od_s, hid_pair, s_flat, chunks, grads, map_acc, map_s, map_r,
    za_s, za_r, yb_s, yb_r, ya_r, zb_r, q_s, q_r, t_ref, t_s1, t_r1, t_mid, t_s2, t_r2, t_s3, t_r3, t_all, t_far,
    acc_a, acc_b, mid,
    hw_sem, f_sem, p_ss, p_rs, m_ss, m_rs,
    za_ss, za_rs, yb_ss, yb_rs, ya_ss, ya_rs, zb_ss, zb_rs, q_ss, q_rs, t_ss, t_rs,
):
    x, z, y, c = place()
    s = lax.axis_index("space")

    def at_z(step):
        return {"dp": index_of(x, (z + step + 8) % 8, y, c)}

    def at_y(step):
        return {"dp": index_of(x, z, (y + step + 4) % 4, c)}

    at_x = {"dp": index_of(1 - x, z, y, c)}
    at_c = {"dp": index_of(x, z, y, 1 - c)}
    at_xc = {"dp": index_of(1 - x, z, y, 1 - c)}
    at_s = {"space": 1 - s}

    load_hw = pltpu.make_async_copy(hw_hbm, hw_ref, hw_sem)
    load_hw.start()
    barrier = pltpu.get_barrier_semaphore()
    peers = [at_s, at_c] + [at_z(k) for k in range(1, 8)] + [at_y(k) for k in range(1, 4)] + [at_x, at_xc]
    for peer in peers:
        pl.semaphore_signal(barrier, inc=1, device_id=peer, device_id_type=MESH)

    copies = []

    def one(src, dst, ssem, rsem, peer):
        copy = pltpu.make_async_remote_copy(
            src_ref=src, dst_ref=dst, send_sem=ssem, recv_sem=rsem, device_id=peer, device_id_type=MESH
        )
        copy.start()
        copies.append(copy)
        return copy

    flat[CELLS:HALF] = jnp.zeros((HALF - CELLS, CHANNELS), F32)
    for row in range(ROWS):
        flat[row * COLS:(row + 1) * COLS] = fm_ref[row].astype(F32)
    feat[0:HALF] = flat[...].astype(BF)
    lane = lax.broadcasted_iota(jnp.int32, (ROIS, 128), 1).astype(F32)
    base = (ROWS * s).astype(F32)
    row_at = jnp.where(lane < ROWS, lane + base, lane - base)
    spot = lax.broadcasted_iota(jnp.int32, (128, HALF), 1).astype(F32)
    slot_at = lax.broadcasted_iota(jnp.int32, (128, HALF), 0).astype(F32)
    row_of = jnp.floor((spot + 0.5) * (1.0 / COLS))
    inside = spot < CELLS
    row_pick = [
        jnp.logical_and(row_of + first == slot_at, inside).astype(F32).astype(BF) for first in (0, ROWS)
    ]
    col_pick = jnp.logical_and(spot - row_of * COLS == slot_at, inside).astype(F32).astype(BF)

    edges = corner_ref[...].astype(F32)
    edges = jnp.transpose(jnp.concatenate([edges, edges], axis=0))

    def bins(low, high, grid, k):
        start = edges[:, low:low + 1]
        size = (edges[:, high:high + 1] - start) / POOL
        total = jnp.zeros((ROIS, 128), F32)
        for offset in (0.25, 0.75):
            point = start + (k + offset) * size - 0.5
            total = total + jnp.maximum(0.0, 1.0 - jnp.abs(point - grid))
        return (0.5 * total).astype(BF)

    for k in range(POOL):
        rows = bins(0, 2, row_at, k)
        for half in range(2):
            row_all[k, :, half * HALF:(half + 1) * HALF] = jnp.dot(
                rows, row_pick[half], preferred_element_type=F32
            ).astype(BF)
        col_all[k] = jnp.dot(bins(1, 3, lane, k), col_pick, preferred_element_type=F32).astype(BF)

    pl.semaphore_wait(barrier, len(peers))
    features = [
        one(feat.at[low:high], feat.at[HALF + low:HALF + high], f_sem.at[k], f_sem.at[2 + k], at_s)
        for k, (low, high) in enumerate(((0, FIRST), (FIRST, HALF)))
    ]

    def build(i, half, low=0, high=HALF):
        at = half * HALF
        for j in range(POOL):
            weights[j * ROIS:(j + 1) * ROIS, low:high] = (
                col_all[j, :, low:high] * row_all[i, :, at + low:at + high]
            )
        return weights[:, low:high]

    def held(i, k):
        return pl.ds(pl.multiple_of((k * POOL + i) * BINS, BINS), BINS)

    def near_part(i, _):
        value = jnp.dot(build(i, 0), feat[0:HALF], preferred_element_type=F32)
        for k in range(2):
            s_flat[held(i, k)] = value[:, k * 128:(k + 1) * 128]
        return 0

    def far_first(i, _):
        value = jnp.dot(build(i, 1, 0, FIRST), feat[HALF:HALF + FIRST], preferred_element_type=F32)
        for k in range(2):
            s_flat[held(i, k)] += value[:, k * 128:(k + 1) * 128]
        return 0

    lax.fori_loop(0, POOL, near_part, 0)
    features[0].wait_recv()
    lax.fori_loop(0, POOL, far_first, 0)
    features[1].wait_recv()
    load_hw.wait()
    hid_acc[...] = jnp.zeros((ROIS, CHANNELS), F32)

    def share(i):
        return pltpu.make_async_remote_copy(
            src_ref=pooled.at[i, 0:ROIS], dst_ref=pooled.at[i, ROIS:2 * ROIS],
            send_sem=p_ss.at[i], recv_sem=p_rs.at[i], device_id=at_c, device_id_type=MESH,
        )

    def far_part(i, _):
        value = jnp.dot(build(i, 1, FIRST, HALF), feat[HALF + FIRST:2 * HALF], preferred_element_type=F32)
        near = [s_flat[held(i, k)] for k in range(2)]
        value = (value + jnp.concatenate(near, axis=1)).astype(BF)
        for j in range(POOL):
            pooled[i, 0:ROIS, j * CHANNELS:(j + 1) * CHANNELS] = value[j * ROIS:(j + 1) * ROIS]
        share(i).start()
        hid_acc[...] += jnp.dot(
            pooled[i, 0:ROIS], hw_ref[pl.ds(pl.multiple_of(i * WIDE, WIDE), WIDE)], preferred_element_type=F32
        )
        return 0

    lax.fori_loop(0, POOL, far_part, 0)

    pre_hidden = hid_acc[...]
    hidden = gelu_of(pre_hidden).astype(BF)
    part = jnp.dot(hidden, ow_ref[...], preferred_element_type=F32)
    z_s[...] = part.astype(BF)
    swap_z = one(z_s, z_r, m_ss.at[0], m_rs.at[0], at_s)
    hid_pair[0:ROIS] = hidden
    send_hid = one(hid_pair.at[0:ROIS], hid_pair.at[ROIS:2 * ROIS], m_ss.at[1], m_rs.at[1], at_c)
    slope = gelu_slope(pre_hidden)
    swap_z.wait_recv()
    pre_output = part + z_r[...].astype(F32)
    delta = (up_ref[...].astype(F32) * gelu_slope(pre_output)).astype(BF)
    od_pair[0:ROIS] = jnp.where(c == 0, delta[:, 0:256], delta[:, 256:512])
    od_s[...] = jnp.where(c == 0, delta[:, 256:512], delta[:, 0:256])
    send_od = one(od_s, od_pair.at[ROIS:2 * ROIS], m_ss.at[2], m_rs.at[2], at_c)
    back = lax.dot_general(delta, ow_ref[...], NT, preferred_element_type=F32)
    hidden_delta = (back * slope).astype(BF)
    hd_own[...] = hidden_delta
    hd_pair[0:ROIS] = jnp.where(c == 0, hidden_delta[:, 0:128], hidden_delta[:, 128:256])
    hd_s[...] = jnp.where(c == 0, hidden_delta[:, 128:256], hidden_delta[:, 0:128])
    send_hd = one(hd_s, hd_pair.at[ROIS:2 * ROIS], m_ss.at[3], m_rs.at[3], at_c)

    def wait_share(i, _):
        share(i).wait_recv()
        return 0

    send_hid.wait_recv()
    send_od.wait_recv()
    second = lax.dot_general(hid_pair[...], od_pair[...], TN, preferred_element_type=F32)
    t_ref[...] = second.reshape(4, 8, 8, 256)
    t_s1[...] = t_ref[...].astype(BF)

    def to_rows():
        return [one(t_s1.at[(y + k) % 4], t_r1.at[k - 1], t_ss.at[k - 1], t_rs.at[k - 1], at_y(k)) for k in range(1, 4)]

    rows_moved = to_rows()
    lax.fori_loop(0, POOL, wait_share, 0)
    send_hd.wait_recv()

    def weight_part(i, _):
        s_flat[pl.ds(pl.multiple_of(i * WIDE, WIDE), WIDE)] = lax.dot_general(
            pooled[i], hd_pair[...], TN, preferred_element_type=F32
        )
        return 0

    def regroup(k, _):
        value = jnp.concatenate([s_flat[pl.ds(k * 196, 196)], jnp.zeros((4, 128), F32)], axis=0)
        chunks[k // 32, (k // 4) % 8, k % 4] = value.astype(BF)
        return 0


    def ring(size, pos, to, own, send, recv, ssem, rsem):
        chains = chains_of(size // 2)
        live = {}

        def slot(k, h):
            return sum(ch[2] for ch in chains[:k]) + h

        def go(k, h):
            u, way, hops = chains[k]
            at = slot(k, h)
            source = own(u, (pos + way * (hops - h) + size) % size)
            if h > 0:
                live[k, h - 1].wait_recv()
                send[at] = source[...] + recv[at - 1]
                source = send.at[at]
            live[k, h] = one(source, recv.at[at], ssem.at[at], rsem.at[at], to(way))

        def total(u):
            value = own(u, pos)[...].astype(F32)
            for k, (piece, _, hops) in enumerate(chains):
                if piece == u and hops > 0:
                    live[k, hops - 1].wait_recv()
                    value = value + recv[slot(k, hops - 1)].astype(F32)
            return value

        return go, total

    za_go, za_total = ring(8, z, at_z, lambda u, d: chunks.at[u, d, :, 0:96, :], za_s, za_r, za_ss, za_rs)
    yb_go, yb_total = ring(4, y, at_y, lambda u, d: chunks.at[u, :, d, 96:200, :], yb_s, yb_r, yb_ss, yb_rs)
    def direct(size, pos, to, acc, recv, ssem, rsem):
        moved = {}

        def go(u):
            for k in range(1, size):
                at = u * (size - 1) + k - 1
                moved[u, k] = one(acc.at[u, (pos + k) % size], recv.at[at], ssem.at[at], rsem.at[at], to(k))

        def total(u):
            value = acc[u, pos].astype(F32)
            for k in range(1, size):
                moved[u, k].wait_recv()
                value = value + recv[u * (size - 1) + k - 1].astype(F32)
            return value

        return go, total

    ya_go, ya_total = direct(4, y, at_y, acc_a, ya_r, ya_ss, ya_rs)
    zb_go, zb_total = direct(8, z, at_z, acc_b, zb_r, zb_ss, zb_rs)

    def take_rows():
        for copy in rows_moved:
            copy.wait_recv()
        t_mid[...] = t_ref[y] + (t_r1[0].astype(F32) + t_r1[1].astype(F32) + t_r1[2].astype(F32))
        t_s2[...] = t_mid[...].astype(BF)
        return [one(t_s2.at[(z + k) % 8], t_r2.at[k - 1], t_ss.at[k + 2], t_rs.at[k + 2], at_z(k)) for k in range(1, 8)]

    def take_cells(moved):
        for copy in moved:
            copy.wait_recv()
        total = t_mid[z]
        for k in range(7):
            total = total + t_r2[k].astype(F32)
        t_s3[...] = total.astype(BF)
        return one(t_s3, t_r3, t_ss.at[10], t_rs.at[10], at_x)

    def take_pair(moved):
        moved.wait_recv()
        t_all[y, z] = (t_s3[...].astype(F32) + t_r3[...].astype(F32)).astype(BF)
        mine = t_all.at[y, z]
        return [one(mine, mine, t_ss.at[10 + k], t_rs.at[10 + k], at_z(k)) for k in range(1, 8)]

    def spread_rows(moved):
        for copy in moved:
            copy.wait_recv()
        mine = t_all.at[y]
        return [one(mine, mine, t_ss.at[17 + k], t_rs.at[17 + k], at_y(k)) for k in range(1, 4)]

    def spread_core(moved):
        for copy in moved:
            copy.wait_recv()
        return one(t_all, t_far, t_ss.at[21], t_rs.at[21], at_c)

    def back_part(half):
        at = half * HALF

        def body(i, _):
            if half == 1:
                g = lax.dot_general(
                    hw_ref[pl.ds(pl.multiple_of(i * WIDE, WIDE), WIDE)], hd_own[...], NT, preferred_element_type=F32
                ).astype(BF)
                for j in range(POOL):
                    grads[i, :, j * ROIS:(j + 1) * ROIS] = g[j * CHANNELS:(j + 1) * CHANNELS]
            map_acc[:, at:at + HALF] += jnp.dot(grads[i], build(i, half), preferred_element_type=F32)
            return 0

        return body

    def work(half, low, high):
        lax.fori_loop(low, high, back_part(half), 0)

    lax.fori_loop(0, 4, weight_part, 0)
    lax.fori_loop(0, 32, regroup, 0)
    za_go(0, 0)
    yb_go(0, 0)
    za_go(2, 0)
    yb_go(2, 0)
    cells_moved = take_rows()
    lax.fori_loop(4, POOL, weight_part, 0)
    lax.fori_loop(32, 64, regroup, 0)
    za_go(1, 0)
    yb_go(1, 0)
    za_go(3, 0)
    map_acc[...] = jnp.zeros((CHANNELS, 2 * HALF), F32)
    za_go(0, 1)
    za_go(2, 1)
    work(1, 0, 1)
    yb_go(0, 1)
    yb_go(3, 0)
    pair_moved = take_cells(cells_moved)
    za_go(1, 1)
    za_go(3, 1)
    za_go(0, 2)
    za_go(2, 2)
    work(1, 1, 3)
    yb_go(1, 1)
    cell_moved = take_pair(pair_moved)
    za_go(1, 2)
    za_go(3, 2)
    za_go(0, 3)
    work(1, 3, 5)
    acc_b[0] = yb_total(0).astype(BF)
    zb_go(0)
    za_go(1, 3)
    row_moved = spread_rows(cell_moved)
    work(1, 5, 7)
    map_s[...] = jnp.transpose(map_acc[:, HALF:2 * HALF]).astype(BF)
    swap_map = one(map_s, map_r, m_ss.at[4], m_rs.at[4], at_s)
    acc_b[1] = yb_total(1).astype(BF)
    zb_go(1)
    for u in (0, 1):
        acc_a[u] = za_total(u).astype(BF)
        ya_go(u)
    core_moved = spread_core(row_moved)
    work(0, 0, 7)
    near = jnp.transpose(map_acc[:, 0:HALF])
    for u in (0, 1):
        mid[u, 0:96] = ya_total(u)
        mid[u, 96:200] = zb_total(u)
    for u in (0, 1):
        for k in (0, 1):
            q_s[u, k] = mid[u, 98 * k:98 * k + 98].astype(BF)
    ends = [
        one(q_s.at[u, k], q_r.at[n], q_ss.at[n], q_rs.at[n], peer)
        for n, (u, k, peer) in enumerate(((1 - x, c, at_x), (x, 1 - c, at_c), (1 - x, 1 - c, at_xc)))
    ]
    swap_map.wait_recv()
    whole = near + map_r[...].astype(F32)
    for k in range(2):
        map_ref[pl.ds(k, CELLS, stride=2), :] = whole[0:CELLS, k * 128:(k + 1) * 128]
    for copy in ends:
        copy.wait_recv()
    mine = q_s[x, c].astype(F32) + q_r[0].astype(F32)
    others = q_r[1].astype(F32) + q_r[2].astype(F32)
    first_ref[:, 0:128] = jnp.where(c == 0, mine, others)
    first_ref[:, 128:256] = jnp.where(c == 0, others, mine)
    core_moved.wait_recv()
    here = t_all[...].astype(F32).reshape(256, 256)
    there = t_far[...].astype(F32).reshape(256, 256)
    second_ref[:, 0:256] = jnp.where(c == 0, here, there)
    second_ref[:, 256:512] = jnp.where(c == 0, there, here)
    for copy in copies:
        copy.wait_send()

    def sent(i, _):
        share(i).wait_send()
        return 0

    lax.fori_loop(0, POOL, sent, 0)


def hand_over(first_ref, second_ref, map_ref, first_out, second_out, map_out):
    first_out[...] = first_ref[...]
    second_out[...] = second_ref[...]
    map_out[...] = map_ref[...]


def on_device(feature_map, proposals, hidden_weight, output_weight, upstream):
    dma = pltpu.SemaphoreType.DMA
    vmem = pl.BlockSpec(memory_space=pltpu.VMEM)
    first, second, grad = pl.pallas_call(
        step_kernel,
        out_shape=(
            jax.ShapeDtypeStruct((98, 256), F32),
            jax.ShapeDtypeStruct((256, 512), F32),
            jax.ShapeDtypeStruct((2 * ROWS * COLS, 128), F32),
        ),
        in_specs=[vmem, vmem, pl.BlockSpec(memory_space=pl.ANY), vmem, vmem],
        out_specs=[vmem] * 3,
        scratch_shapes=[
            pltpu.VMEM((POOL * WIDE, 256), BF),
            pltpu.VMEM((2 * HALF, CHANNELS), BF),
            pltpu.VMEM((HALF, CHANNELS), F32),
            pltpu.VMEM((POOL, ROIS, 2 * HALF), BF),
            pltpu.VMEM((POOL, ROIS, HALF), BF),
            pltpu.VMEM((BINS, HALF), BF),
            pltpu.VMEM((POOL, 2 * ROIS, WIDE), BF),
            pltpu.VMEM((ROIS, CHANNELS), F32),
            pltpu.VMEM((ROIS, 512), BF), pltpu.VMEM((ROIS, 512), BF),
            pltpu.VMEM((ROIS, 256), BF),
            pltpu.VMEM((2 * ROIS, 128), BF), pltpu.VMEM((ROIS, 128), BF),
            pltpu.VMEM((2 * ROIS, 256), BF), pltpu.VMEM((ROIS, 256), BF),
            pltpu.VMEM((2 * ROIS, 256), BF),
            pltpu.VMEM((POOL * WIDE, 128), F32),
            pltpu.VMEM((2, 8, 4, 200, 128), BF),
            pltpu.VMEM((POOL, CHANNELS, BINS), BF),
            pltpu.VMEM((CHANNELS, 2 * HALF), F32),
            pltpu.VMEM((HALF, CHANNELS), BF), pltpu.VMEM((HALF, CHANNELS), BF),
            pltpu.VMEM((14, 4, 96, 128), BF), pltpu.VMEM((14, 4, 96, 128), BF),
            pltpu.VMEM((6, 8, 104, 128), BF), pltpu.VMEM((6, 8, 104, 128), BF),
            pltpu.VMEM((6, 96, 128), BF),
            pltpu.VMEM((14, 104, 128), BF),
            pltpu.VMEM((2, 2, 98, 128), BF), pltpu.VMEM((3, 98, 128), BF),
            pltpu.VMEM((4, 8, 8, 256), F32), pltpu.VMEM((4, 8, 8, 256), BF), pltpu.VMEM((3, 8, 8, 256), BF),
            pltpu.VMEM((8, 8, 256), F32), pltpu.VMEM((8, 8, 256), BF), pltpu.VMEM((7, 8, 256), BF),
            pltpu.VMEM((8, 256), BF), pltpu.VMEM((8, 256), BF),
            pltpu.VMEM((4, 8, 8, 256), BF), pltpu.VMEM((4, 8, 8, 256), BF),
            pltpu.VMEM((2, 4, 96, 128), BF), pltpu.VMEM((2, 8, 104, 128), BF),
            pltpu.VMEM((2, 200, 128), F32),
            dma(()), dma((4,)), dma((POOL,)), dma((POOL,)), dma((5,)), dma((5,)),
            dma((14,)), dma((14,)), dma((6,)), dma((6,)), dma((6,)), dma((6,)), dma((14,)), dma((14,)),
            dma((3,)), dma((3,)), dma((22,)), dma((22,)),
        ],
        compiler_params=pltpu.CompilerParams(
            collective_id=1, has_side_effects=True, vmem_limit_bytes=67043328
        ),
        name="box_head_step",
    )(feature_map[0], jnp.transpose(proposals[0]), hidden_weight, output_weight, upstream[0])
    first, second, grad = pl.pallas_call(
        hand_over,
        out_shape=tuple(jax.ShapeDtypeStruct(v.shape, v.dtype) for v in (first, second, grad)),
        in_specs=[vmem] * 3,
        out_specs=[vmem] * 3,
        name="hand_over",
    )(first, second, grad)
    return (first, second, grad.reshape(1, ROWS, COLS, CHANNELS))


def solution(mesh):
    placed = (
        P("dp", "space", None, None),
        P("dp", None, None),
        P(None, "space"),
        P("space", None),
        P("dp", None, None),
    )
    return jax.shard_map(
        on_device,
        mesh=mesh,
        in_specs=placed,
        out_specs=(P("dp", "space"), P("space", None), P("dp", "space", None, None)),
        check_vma=False,
    )
```

```python
import jax
import jax.numpy as jnp
from jax import lax
from jax.experimental import pallas as pl
from jax.experimental.pallas import tpu as pltpu
from jax.sharding import PartitionSpec as P

MESH = pl.DeviceIdType.MESH
POOL = 7
ROIS = 128
CHANNELS = 256
ROWS = 12
COLS = 84
CELLS = ROWS * COLS
HALF = 1024
FIRST = 768
EARLY = 3
BINS = POOL * ROIS
WIDE = POOL * CHANNELS
BF = jnp.bfloat16
F32 = jnp.float32
TN = (((0,), (0,)), ((), ()))
NT = (((1,), (1,)), ((), ()))
SCALE = 0.7978845608028654
CUBIC = 0.044715


def gelu_of(v):
    return 0.5 * v * (1.0 + jnp.tanh(SCALE * (v + CUBIC * v * v * v)))


def gelu_slope(v):
    t = jnp.tanh(SCALE * (v + CUBIC * v * v * v))
    return 0.5 * (1.0 + t) + 0.5 * v * (1.0 - t * t) * (SCALE * (1.0 + 3.0 * CUBIC * v * v))


def place():
    me = lax.axis_index("dp")
    return me // 64, (me // 8) % 8, (me // 2) % 4, me % 2


def index_of(x, z, y, c):
    return ((x * 8 + z) * 4 + y) * 2 + c


def chains_of(hops):
    return ((0, 1, hops), (1, -1, hops), (0, -1, hops - 1), (1, 1, hops - 1))


def step_kernel(
    fm_ref, corner_ref, hw_hbm, ow_ref, up_ref, first_ref, second_ref, map_ref,
    hw_ref, feat, flat, row_all, col_all, weights, pooled, hid_acc,
    z_s, z_r, hd_own, hd_pair, hd_s, od_pair, od_s, hid_pair, s_flat, chunks, grads, map_acc, map_s, map_r,
    za_s, za_r, yb_s, yb_r, ya_r, zb_r, q_s, q_r, t_ref, t_s1, t_r1, t_mid, t_s2, t_r2, t_s3, t_r3, t_all, t_far,
    acc_a, acc_b, mid,
    hw_sem, f_sem, p_ss, p_rs, m_ss, m_rs,
    za_ss, za_rs, yb_ss, yb_rs, ya_ss, ya_rs, zb_ss, zb_rs, q_ss, q_rs, t_ss, t_rs,
):
    x, z, y, c = place()
    s = lax.axis_index("space")

    def at_z(step):
        return {"dp": index_of(x, (z + step + 8) % 8, y, c)}

    def at_y(step):
        return {"dp": index_of(x, z, (y + step + 4) % 4, c)}

    at_x = {"dp": index_of(1 - x, z, y, c)}
    at_c = {"dp": index_of(x, z, y, 1 - c)}
    at_xc = {"dp": index_of(1 - x, z, y, 1 - c)}
    at_s = {"space": 1 - s}

    load_hw = pltpu.make_async_copy(hw_hbm, hw_ref, hw_sem)
    load_hw.start()
    barrier = pltpu.get_barrier_semaphore()
    peers = [at_s, at_c] + [at_z(k) for k in range(1, 8)] + [at_y(k) for k in range(1, 4)] + [at_x, at_xc]
    for peer in peers:
        pl.semaphore_signal(barrier, inc=1, device_id=peer, device_id_type=MESH)

    copies = []

    def one(src, dst, ssem, rsem, peer):
        copy = pltpu.make_async_remote_copy(
            src_ref=src, dst_ref=dst, send_sem=ssem, recv_sem=rsem, device_id=peer, device_id_type=MESH
        )
        copy.start()
        copies.append(copy)
        return copy

    flat[CELLS:HALF] = jnp.zeros((HALF - CELLS, CHANNELS), F32)
    for row in range(ROWS):
        flat[row * COLS:(row + 1) * COLS] = fm_ref[row].astype(F32)
    feat[0:HALF] = flat[...].astype(BF)
    lane = lax.broadcasted_iota(jnp.int32, (ROIS, 128), 1).astype(F32)
    base = (ROWS * s).astype(F32)
    row_at = jnp.where(lane < ROWS, lane + base, lane - base)
    spot = lax.broadcasted_iota(jnp.int32, (128, HALF), 1).astype(F32)
    slot_at = lax.broadcasted_iota(jnp.int32, (128, HALF), 0).astype(F32)
    row_of = jnp.floor((spot + 0.5) * (1.0 / COLS))
    inside = spot < CELLS
    row_pick = [
        jnp.logical_and(row_of + first == slot_at, inside).astype(F32).astype(BF) for first in (0, ROWS)
    ]
    col_pick = jnp.logical_and(spot - row_of * COLS == slot_at, inside).astype(F32).astype(BF)

    edges = corner_ref[...].astype(F32)
    edges = jnp.transpose(jnp.concatenate([edges, edges], axis=0))

    def bins(low, high, grid, k):
        start = edges[:, low:low + 1]
        size = (edges[:, high:high + 1] - start) / POOL
        total = jnp.zeros((ROIS, 128), F32)
        for offset in (0.25, 0.75):
            point = start + (k + offset) * size - 0.5
            total = total + jnp.maximum(0.0, 1.0 - jnp.abs(point - grid))
        return (0.5 * total).astype(BF)

    for k in range(POOL):
        rows = bins(0, 2, row_at, k)
        for half in range(2):
            row_all[k, :, half * HALF:(half + 1) * HALF] = jnp.dot(
                rows, row_pick[half], preferred_element_type=F32
            ).astype(BF)
        col_all[k] = jnp.dot(bins(1, 3, lane, k), col_pick, preferred_element_type=F32).astype(BF)

    pl.semaphore_wait(barrier, len(peers))
    features = [
        one(feat.at[low:high], feat.at[HALF + low:HALF + high], f_sem.at[k], f_sem.at[2 + k], at_s)
        for k, (low, high) in enumerate(((0, FIRST), (FIRST, HALF)))
    ]

    def build(i, half, low=0, high=HALF):
        at = half * HALF
        for j in range(POOL):
            weights[j * ROIS:(j + 1) * ROIS, low:high] = (
                col_all[j, :, low:high] * row_all[i, :, at + low:at + high]
            )
        return weights[:, low:high]

    def held(i, k):
        return pl.ds(pl.multiple_of((k * POOL + i) * BINS, BINS), BINS)

    def near_part(i, _):
        value = jnp.dot(build(i, 0), feat[0:HALF], preferred_element_type=F32)
        for k in range(2):
            s_flat[held(i, k)] = value[:, k * 128:(k + 1) * 128]
        return 0

    def far_first(i, _):
        value = jnp.dot(build(i, 1, 0, FIRST), feat[HALF:HALF + FIRST], preferred_element_type=F32)
        for k in range(2):
            s_flat[held(i, k)] += value[:, k * 128:(k + 1) * 128]
        return 0

    lax.fori_loop(0, POOL, near_part, 0)
    features[0].wait_recv()
    lax.fori_loop(0, EARLY, far_first, 0)
    features[1].wait_recv()
    load_hw.wait()
    hid_acc[...] = jnp.zeros((ROIS, CHANNELS), F32)

    def share(i):
        return pltpu.make_async_remote_copy(
            src_ref=pooled.at[i, 0:ROIS], dst_ref=pooled.at[i, ROIS:2 * ROIS],
            send_sem=p_ss.at[i], recv_sem=p_rs.at[i], device_id=at_c, device_id_type=MESH,
        )

    def far_part(low):
        def body(i, _):
            value = jnp.dot(build(i, 1, low, HALF), feat[HALF + low:2 * HALF], preferred_element_type=F32)
            near = [s_flat[held(i, k)] for k in range(2)]
            value = (value + jnp.concatenate(near, axis=1)).astype(BF)
            for j in range(POOL):
                pooled[i, 0:ROIS, j * CHANNELS:(j + 1) * CHANNELS] = value[j * ROIS:(j + 1) * ROIS]
            share(i).start()
            hid_acc[...] += jnp.dot(
                pooled[i, 0:ROIS], hw_ref[pl.ds(pl.multiple_of(i * WIDE, WIDE), WIDE)], preferred_element_type=F32
            )
            return 0

        return body

    lax.fori_loop(0, EARLY, far_part(FIRST), 0)
    lax.fori_loop(EARLY, POOL, far_part(0), 0)

    pre_hidden = hid_acc[...]
    hidden = gelu_of(pre_hidden).astype(BF)
    part = jnp.dot(hidden, ow_ref[...], preferred_element_type=F32)
    z_s[...] = part.astype(BF)
    swap_z = one(z_s, z_r, m_ss.at[0], m_rs.at[0], at_s)
    hid_pair[0:ROIS] = hidden
    send_hid = one(hid_pair.at[0:ROIS], hid_pair.at[ROIS:2 * ROIS], m_ss.at[1], m_rs.at[1], at_c)
    slope = gelu_slope(pre_hidden)
    swap_z.wait_recv()
    pre_output = part + z_r[...].astype(F32)
    delta = (up_ref[...].astype(F32) * gelu_slope(pre_output)).astype(BF)
    od_pair[0:ROIS] = jnp.where(c == 0, delta[:, 0:256], delta[:, 256:512])
    od_s[...] = jnp.where(c == 0, delta[:, 256:512], delta[:, 0:256])
    send_od = one(od_s, od_pair.at[ROIS:2 * ROIS], m_ss.at[2], m_rs.at[2], at_c)
    back = lax.dot_general(delta, ow_ref[...], NT, preferred_element_type=F32)
    hidden_delta = (back * slope).astype(BF)
    hd_own[...] = hidden_delta
    hd_pair[0:ROIS] = jnp.where(c == 0, hidden_delta[:, 0:128], hidden_delta[:, 128:256])
    hd_s[...] = jnp.where(c == 0, hidden_delta[:, 128:256], hidden_delta[:, 0:128])
    send_hd = one(hd_s, hd_pair.at[ROIS:2 * ROIS], m_ss.at[3], m_rs.at[3], at_c)

    def wait_share(i, _):
        share(i).wait_recv()
        return 0

    send_hid.wait_recv()
    send_od.wait_recv()
    second = lax.dot_general(hid_pair[...], od_pair[...], TN, preferred_element_type=F32)
    t_ref[...] = second.reshape(4, 8, 8, 256)
    t_s1[...] = t_ref[...].astype(BF)

    def to_rows():
        return [one(t_s1.at[(y + k) % 4], t_r1.at[k - 1], t_ss.at[k - 1], t_rs.at[k - 1], at_y(k)) for k in range(1, 4)]

    rows_moved = to_rows()
    lax.fori_loop(0, POOL, wait_share, 0)
    send_hd.wait_recv()

    def weight_part(i, _):
        s_flat[pl.ds(pl.multiple_of(i * WIDE, WIDE), WIDE)] = lax.dot_general(
            pooled[i], hd_pair[...], TN, preferred_element_type=F32
        )
        return 0

    def regroup(k, _):
        value = jnp.concatenate([s_flat[pl.ds(k * 196, 196)], jnp.zeros((4, 128), F32)], axis=0)
        chunks[k // 32, (k // 4) % 8, k % 4] = value.astype(BF)
        return 0


    def ring(size, pos, to, own, send, recv, ssem, rsem):
        chains = chains_of(size // 2)
        live = {}

        def slot(k, h):
            return sum(ch[2] for ch in chains[:k]) + h

        def go(k, h):
            u, way, hops = chains[k]
            at = slot(k, h)
            source = own(u, (pos + way * (hops - h) + size) % size)
            if h > 0:
                live[k, h - 1].wait_recv()
                send[at] = source[...] + recv[at - 1]
                source = send.at[at]
            live[k, h] = one(source, recv.at[at], ssem.at[at], rsem.at[at], to(way))

        def total(u):
            value = own(u, pos)[...].astype(F32)
            for k, (piece, _, hops) in enumerate(chains):
                if piece == u and hops > 0:
                    live[k, hops - 1].wait_recv()
                    value = value + recv[slot(k, hops - 1)].astype(F32)
            return value

        return go, total

    za_go, za_total = ring(8, z, at_z, lambda u, d: chunks.at[u, d, :, 0:96, :], za_s, za_r, za_ss, za_rs)
    yb_go, yb_total = ring(4, y, at_y, lambda u, d: chunks.at[u, :, d, 96:200, :], yb_s, yb_r, yb_ss, yb_rs)
    def direct(size, pos, to, acc, recv, ssem, rsem):
        moved = {}

        def go(u):
            for k in range(1, size):
                at = u * (size - 1) + k - 1
                moved[u, k] = one(acc.at[u, (pos + k) % size], recv.at[at], ssem.at[at], rsem.at[at], to(k))

        def total(u):
            value = acc[u, pos].astype(F32)
            for k in range(1, size):
                moved[u, k].wait_recv()
                value = value + recv[u * (size - 1) + k - 1].astype(F32)
            return value

        return go, total

    ya_go, ya_total = direct(4, y, at_y, acc_a, ya_r, ya_ss, ya_rs)
    zb_go, zb_total = direct(8, z, at_z, acc_b, zb_r, zb_ss, zb_rs)

    def take_rows():
        for copy in rows_moved:
            copy.wait_recv()
        t_mid[...] = t_ref[y] + (t_r1[0].astype(F32) + t_r1[1].astype(F32) + t_r1[2].astype(F32))
        t_s2[...] = t_mid[...].astype(BF)
        return [one(t_s2.at[(z + k) % 8], t_r2.at[k - 1], t_ss.at[k + 2], t_rs.at[k + 2], at_z(k)) for k in range(1, 8)]

    def take_cells(moved):
        for copy in moved:
            copy.wait_recv()
        total = t_mid[z]
        for k in range(7):
            total = total + t_r2[k].astype(F32)
        t_s3[...] = total.astype(BF)
        return one(t_s3, t_r3, t_ss.at[10], t_rs.at[10], at_x)

    def take_pair(moved):
        moved.wait_recv()
        t_all[y, z] = (t_s3[...].astype(F32) + t_r3[...].astype(F32)).astype(BF)
        mine = t_all.at[y, z]
        return [one(mine, mine, t_ss.at[10 + k], t_rs.at[10 + k], at_z(k)) for k in range(1, 8)]

    def spread_rows(moved):
        for copy in moved:
            copy.wait_recv()
        mine = t_all.at[y]
        return [one(mine, mine, t_ss.at[17 + k], t_rs.at[17 + k], at_y(k)) for k in range(1, 4)]

    def spread_core(moved):
        for copy in moved:
            copy.wait_recv()
        return one(t_all, t_far, t_ss.at[21], t_rs.at[21], at_c)

    def back_part(half):
        at = half * HALF

        def body(i, _):
            if half == 1:
                g = lax.dot_general(
                    hw_ref[pl.ds(pl.multiple_of(i * WIDE, WIDE), WIDE)], hd_own[...], NT, preferred_element_type=F32
                ).astype(BF)
                for j in range(POOL):
                    grads[i, :, j * ROIS:(j + 1) * ROIS] = g[j * CHANNELS:(j + 1) * CHANNELS]
            map_acc[:, at:at + HALF] += jnp.dot(grads[i], build(i, half), preferred_element_type=F32)
            return 0

        return body

    def work(half, low, high):
        lax.fori_loop(low, high, back_part(half), 0)

    lax.fori_loop(0, 4, weight_part, 0)
    lax.fori_loop(0, 32, regroup, 0)
    za_go(0, 0)
    yb_go(0, 0)
    za_go(2, 0)
    yb_go(2, 0)
    cells_moved = take_rows()
    lax.fori_loop(4, POOL, weight_part, 0)
    lax.fori_loop(32, 64, regroup, 0)
    za_go(1, 0)
    yb_go(1, 0)
    za_go(3, 0)
    map_acc[...] = jnp.zeros((CHANNELS, 2 * HALF), F32)
    za_go(0, 1)
    za_go(2, 1)
    work(1, 0, 1)
    yb_go(0, 1)
    yb_go(3, 0)
    za_go(1, 1)
    za_go(3, 1)
    za_go(0, 2)
    za_go(2, 2)
    pair_moved = take_cells(cells_moved)
    work(1, 1, 3)
    yb_go(1, 1)
    cell_moved = take_pair(pair_moved)
    za_go(1, 2)
    za_go(3, 2)
    za_go(0, 3)
    work(1, 3, 5)
    acc_b[0] = yb_total(0).astype(BF)
    zb_go(0)
    za_go(1, 3)
    row_moved = spread_rows(cell_moved)
    work(1, 5, 7)
    map_s[...] = jnp.transpose(map_acc[:, HALF:2 * HALF]).astype(BF)
    swap_map = one(map_s, map_r, m_ss.at[4], m_rs.at[4], at_s)
    acc_b[1] = yb_total(1).astype(BF)
    zb_go(1)
    for u in (0, 1):
        acc_a[u] = za_total(u).astype(BF)
        ya_go(u)
    core_moved = spread_core(row_moved)
    work(0, 0, 7)
    near = jnp.transpose(map_acc[:, 0:HALF])
    for u in (0, 1):
        mid[u, 0:96] = ya_total(u)
        mid[u, 96:200] = zb_total(u)
    for u in (0, 1):
        for k in (0, 1):
            q_s[u, k] = mid[u, 98 * k:98 * k + 98].astype(BF)
    ends = [
        one(q_s.at[u, k], q_r.at[n], q_ss.at[n], q_rs.at[n], peer)
        for n, (u, k, peer) in enumerate(((1 - x, c, at_x), (x, 1 - c, at_c), (1 - x, 1 - c, at_xc)))
    ]
    core_moved.wait_recv()
    here = t_all[...].astype(F32).reshape(256, 256)
    there = t_far[...].astype(F32).reshape(256, 256)
    second_ref[:, 0:256] = jnp.where(c == 0, here, there)
    second_ref[:, 256:512] = jnp.where(c == 0, there, here)
    swap_map.wait_recv()
    whole = near + map_r[...].astype(F32)
    for k in range(2):
        map_ref[pl.ds(k, CELLS, stride=2), :] = whole[0:CELLS, k * 128:(k + 1) * 128]
    for copy in ends:
        copy.wait_recv()
    mine = q_s[x, c].astype(F32) + q_r[0].astype(F32)
    others = q_r[1].astype(F32) + q_r[2].astype(F32)
    first_ref[:, 0:128] = jnp.where(c == 0, mine, others)
    first_ref[:, 128:256] = jnp.where(c == 0, others, mine)
    for copy in copies:
        copy.wait_send()

    def sent(i, _):
        share(i).wait_send()
        return 0

    lax.fori_loop(0, POOL, sent, 0)


def hand_over(first_ref, second_ref, map_ref, first_out, second_out, map_out):
    first_out[...] = first_ref[...]
    second_out[...] = second_ref[...]
    map_out[...] = map_ref[...]


def on_device(feature_map, proposals, hidden_weight, output_weight, upstream):
    dma = pltpu.SemaphoreType.DMA
    vmem = pl.BlockSpec(memory_space=pltpu.VMEM)
    first, second, grad = pl.pallas_call(
        step_kernel,
        out_shape=(
            jax.ShapeDtypeStruct((98, 256), F32),
            jax.ShapeDtypeStruct((256, 512), F32),
            jax.ShapeDtypeStruct((2 * ROWS * COLS, 128), F32),
        ),
        in_specs=[vmem, vmem, pl.BlockSpec(memory_space=pl.ANY), vmem, vmem],
        out_specs=[vmem] * 3,
        scratch_shapes=[
            pltpu.VMEM((POOL * WIDE, 256), BF),
            pltpu.VMEM((2 * HALF, CHANNELS), BF),
            pltpu.VMEM((HALF, CHANNELS), F32),
            pltpu.VMEM((POOL, ROIS, 2 * HALF), BF),
            pltpu.VMEM((POOL, ROIS, HALF), BF),
            pltpu.VMEM((BINS, HALF), BF),
            pltpu.VMEM((POOL, 2 * ROIS, WIDE), BF),
            pltpu.VMEM((ROIS, CHANNELS), F32),
            pltpu.VMEM((ROIS, 512), BF), pltpu.VMEM((ROIS, 512), BF),
            pltpu.VMEM((ROIS, 256), BF),
            pltpu.VMEM((2 * ROIS, 128), BF), pltpu.VMEM((ROIS, 128), BF),
            pltpu.VMEM((2 * ROIS, 256), BF), pltpu.VMEM((ROIS, 256), BF),
            pltpu.VMEM((2 * ROIS, 256), BF),
            pltpu.VMEM((POOL * WIDE, 128), F32),
            pltpu.VMEM((2, 8, 4, 200, 128), BF),
            pltpu.VMEM((POOL, CHANNELS, BINS), BF),
            pltpu.VMEM((CHANNELS, 2 * HALF), F32),
            pltpu.VMEM((HALF, CHANNELS), BF), pltpu.VMEM((HALF, CHANNELS), BF),
            pltpu.VMEM((14, 4, 96, 128), BF), pltpu.VMEM((14, 4, 96, 128), BF),
            pltpu.VMEM((6, 8, 104, 128), BF), pltpu.VMEM((6, 8, 104, 128), BF),
            pltpu.VMEM((6, 96, 128), BF),
            pltpu.VMEM((14, 104, 128), BF),
            pltpu.VMEM((2, 2, 98, 128), BF), pltpu.VMEM((3, 98, 128), BF),
            pltpu.VMEM((4, 8, 8, 256), F32), pltpu.VMEM((4, 8, 8, 256), BF), pltpu.VMEM((3, 8, 8, 256), BF),
            pltpu.VMEM((8, 8, 256), F32), pltpu.VMEM((8, 8, 256), BF), pltpu.VMEM((7, 8, 256), BF),
            pltpu.VMEM((8, 256), BF), pltpu.VMEM((8, 256), BF),
            pltpu.VMEM((4, 8, 8, 256), BF), pltpu.VMEM((4, 8, 8, 256), BF),
            pltpu.VMEM((2, 4, 96, 128), BF), pltpu.VMEM((2, 8, 104, 128), BF),
            pltpu.VMEM((2, 200, 128), F32),
            dma(()), dma((4,)), dma((POOL,)), dma((POOL,)), dma((5,)), dma((5,)),
            dma((14,)), dma((14,)), dma((6,)), dma((6,)), dma((6,)), dma((6,)), dma((14,)), dma((14,)),
            dma((3,)), dma((3,)), dma((22,)), dma((22,)),
        ],
        compiler_params=pltpu.CompilerParams(
            collective_id=1, has_side_effects=True, vmem_limit_bytes=67043328
        ),
        name="box_head_step",
    )(feature_map[0], jnp.transpose(proposals[0]), hidden_weight, output_weight, upstream[0])
    first, second, grad = pl.pallas_call(
        hand_over,
        out_shape=tuple(jax.ShapeDtypeStruct(v.shape, v.dtype) for v in (first, second, grad)),
        in_specs=[vmem] * 3,
        out_specs=[vmem] * 3,
        name="hand_over",
    )(first, second, grad)
    return (first, second, grad.reshape(1, ROWS, COLS, CHANNELS))


def solution(mesh):
    placed = (
        P("dp", "space", None, None),
        P("dp", None, None),
        P(None, "space"),
        P("space", None),
        P("dp", None, None),
    )
    return jax.shard_map(
        on_device,
        mesh=mesh,
        in_specs=placed,
        out_specs=(P("dp", "space"), P("space", None), P("dp", "space", None, None)),
        check_vma=False,
    )
```
